128 devices in a mesh: tok: 16 (over x, y), head: 8 (over z, core).
Axes of the slice: x: 4, y: 4, z: 4, core: 2. Of those that a mesh axis runs over, the one named last changes fastest.
Arguments:
- tokens: bfloat16 [16384, 1536], P(('tok', 'head')), may hold values from -6 to 6
- segments: int32 [16384], replicated, may hold values from 0 to 127, never falling along the last dimension, each value on 1 to 1024 neighbouring positions
- group_ids: int32 [128], replicated, may hold values from 0 to 15
- prefix_owner: int32 [16], replicated, may hold values from 0 to 15, each once
- slab_fill: int32 [16], replicated, may hold values from 256 to 512
- prefix_cache: bfloat16 [8192, 1024], P('tok', 'head'), may hold values from -400 to 400, as said below
- attn_gain: float32 [1536], replicated, may hold values from 0.5 to 1.5
- w_query: bfloat16 [1536, 1536], P(None, 'head'), may hold values from -0.15625 to 0.15625
- w_keyval: bfloat16 [1536, 1024], P(None, 'head'), may hold values from -0.15625 to 0.15625
- w_out: bfloat16 [1536, 1536], P('head'), may hold values from -0.15625 to 0.15625
- ffn_gain: float32 [1536], replicated, may hold values from 0.5 to 1.5
- routes: int32 [16384, 8], P(('tok', 'head')), may hold values from 0 to 31, all different within a row; in each aligned block of 128 rows (0 to 127, 128 to 255, ...) at most 64 rows name the same one
- route_gates: float32 [16384, 8], P(('tok', 'head')), may hold values from 0.05 to 0.5
- w_gate: bfloat16 [32, 1536, 512], P('tok'), may hold values from -0.15625 to 0.15625
- w_up: bfloat16 [32, 1536, 512], P('tok'), may hold values from -0.15625 to 0.15625
- w_down: bfloat16 [32, 512, 1536], P('tok'), may hold values from -0.25 to 0.25
Outputs:
- layer_out: bfloat16 [16384, 1536], P(('tok', 'head'))
The draws below stay inside these ranges and needn't reach their ends.
Inputs may be any that keep to these rules, and one draw needn't show every extreme that they name: `segments`: request ids never fall along the tokens; every request has 1 to 1024 tokens and some request exactly 1024. `prefix_owner`: each group's prefix lies in exactly one slab. `prefix_cache`: keys are already rotated by their positions 0 to fill - 1; rows at fill and past it are padding. `routes`: each row names 8 different experts; the rows of one device name any expert at most 64 times.
All inputs are finite; a program needn't handle non-finite values.
Results may differ from the reference program's by a relative error of at most 0.012.
Values may be sent and summed in bfloat16 or wider, within the bound.
A program may use at most 192 MiB of HBM per device.

```python
import math
import jax
import jax.numpy as jnp
import numpy as np
from jax import lax

D = 1536
HQ = 24
KVH = 8
HS = 64
FF = 512
EXPERTS = 32
TOPK = 8
PREFIX = 512
TOK_DEV = 128
TOK_ROW = 1024
TOKENS = 16384
REQS = 128
GROUPS = 16
CAP = 64


def draw_prefix_cache(key, part):
    base = jax.random.truncated_normal(key, -4.0, 4.0, (GROUPS, PREFIX, KVH, 2, HS), jnp.float32)
    level_key = jax.random.fold_in(key, 11)
    level = jax.random.uniform(level_key, (GROUPS, 1, 1, 1, 1), jnp.float32, math.log(0.5), math.log(2.0))
    factor = jnp.concatenate([jnp.exp(level), jnp.ones((GROUPS, 1, 1, 1, 1), jnp.float32)], axis=3)
    return (base * factor).reshape(GROUPS * PREFIX, KVH * 2 * HS).astype(jnp.bfloat16)


def plant(array, own_key, low, largest):
    spot = [jax.random.randint(jax.random.fold_in(own_key, axis), (), 0, length) for axis, length in enumerate(array.shape)]
    longest = array.shape.index(max(array.shape))
    neighbour = spot[:longest] + [(spot[longest] + 1) % array.shape[longest]] + spot[longest + 1:]
    return array.at[tuple(spot)].set(low).at[tuple(neighbour)].set(largest)


def block_levels(rng, extent, pieces, smallest, top_value):
    level, own = 1.0, jax.random.fold_in(rng, 6)
    for dim, blocks in pieces:
        heights = jnp.exp(jax.random.uniform(jax.random.fold_in(own, dim), (blocks,), jnp.float32, smallest / len(pieces), top_value / len(pieces)))
        level = level * jnp.repeat(heights, extent[dim] // blocks).reshape([-1 if axis == dim else 1 for axis in range(len(extent))])
    return level


def cumulative_ranks(count, slope):
    weights = [(1 << 20) // math.isqrt(grade ** slope) + 1 for grade in range(1, count + 1)]
    scale = 1 + sum(weights) // (1 << 30)
    return np.cumsum(np.array([max(1, weight // scale) for weight in weights]))


def ranked_ids(key, extent, count, slope):
    listing = cumulative_ranks(count, slope)
    lot = jax.random.randint(jax.random.fold_in(key, 1), extent, 0, int(listing[count - 1]))
    grade = jnp.searchsorted(jnp.asarray(listing, jnp.int32), lot, side="right")
    return jax.random.permutation(jax.random.fold_in(key, 2), count)[grade].astype(jnp.int32)


def split_up(number_of, total, most, lean):
    weights = [(1 << 20) // math.isqrt(standing ** lean) + 1 for standing in range(2, number_of + 1)]
    surplus, counts = total - most - (number_of - 1), [1] * (number_of - 1)
    while surplus > 0:
        candidates = [i for i in range(number_of - 1) if counts[i] < most]
        pool, remaining = sum([weights[i] for i in candidates]), surplus
        for i in candidates:
            extra = min(most - counts[i], max(1, remaining * weights[i] // pool), surplus)
            counts[i] = counts[i] + extra
            surplus = surplus - extra
    return np.array([most] + counts)


def ragged(rng, number_of, total, bound, lean):
    if number_of == 2:
        one = jax.random.randint(rng, (), max(1, total - bound), min(bound, total - 1) + 1)
        return jnp.stack([one, total - one])
    sizes = jnp.asarray(split_up(number_of, total, bound, lean), jnp.int32)
    couples = (number_of - 1) // 2
    giver, sink = sizes[1:1 + 2 * couples:2], sizes[2:2 + 2 * couples:2]
    room = jnp.minimum(giver - 1, bound - sink)
    passed = jax.random.randint(jax.random.fold_in(rng, 1), (couples,), 0, 1 << 20) % (room + 1)
    sizes = sizes.at[1:1 + 2 * couples:2].set(giver - passed).at[2:2 + 2 * couples:2].set(sink + passed)
    return sizes[jax.random.permutation(jax.random.fold_in(rng, 2), number_of)]


def shared_out(own_key, own, number, rows, number_of, top, limit, lean):
    sequence = jax.random.permutation(own_key, number_of)
    crowded, common = shares(number_of, rows * top, limit, lean, True), shares(number_of, rows * top, limit, lean, False)
    places = jnp.arange(number_of)

    def named(lengths, rotation):
        used = int((lengths > 0).sum())
        fixed = max(1, used // 4)
        shifted = fixed + (places - fixed + rotation * (used - fixed)) % max(1, number_of - fixed)
        return jnp.zeros((number_of,), jnp.int32).at[sequence[jnp.where(places < fixed, places, shifted)]].set(jnp.asarray(lengths, jnp.int32))

    lengths = jnp.where(number % 4 == 0, named(crowded, number // 4), named(common, number - number // 4 - 1))
    mixed = jax.random.permutation(jax.random.fold_in(own, 3), number_of)
    source_of, sink = mixed[0:number_of // 2 * 2:2], mixed[1:number_of // 2 * 2:2]
    margin = jnp.minimum(lengths[source_of] - 1, limit - lengths[sink]) // 2
    margin = jnp.where((source_of == sequence[0]) | (sink == sequence[0]) | (lengths[sink] == 0), 0, jnp.maximum(margin, 0))
    shifted = jax.random.randint(jax.random.fold_in(own, 4), (number_of // 2,), 0, 1 << 20) % (margin + 1)
    lengths = lengths.at[source_of].add(-shifted).at[sink].add(shifted)
    labels = jnp.searchsorted(jnp.cumsum(lengths), jnp.arange(rows * top), side="right").astype(jnp.int32)
    table = labels.reshape(top, rows).T
    table = table[jax.random.permutation(jax.random.fold_in(own, 1), rows)]
    rotation = jax.random.randint(jax.random.fold_in(own, 2), (rows, 1), 0, top)
    return jnp.take_along_axis(table, (jnp.arange(top)[None, :] + rotation) % top, axis=1)


def shares(amount, total, reach, lean, full):
    portions = [(1 << 20) // math.isqrt(rank ** lean) + 1 for rank in range(1, amount + 1)]
    largest = reach if full else min(reach, max(-(-total // amount), total * portions[0] // sum(portions)))
    least = 1 if total - largest >= amount - 1 else 0
    given, surplus = [largest] + [least] * (amount - 1), total - largest - least * (amount - 1)
    while surplus > 0:
        free = [i for i in range(1, amount) if given[i] < largest] or [i for i in range(1, amount) if given[i] < reach]
        pool, remaining = sum([portions[i] for i in free]), surplus
        for i in free:
            more = min(reach - given[i], max(1, remaining * portions[i] // pool), surplus)
            given[i] = given[i] + more
            surplus = surplus - more
    return np.array(given)


def noise(stream_key, shape, scale, most, shards=(), held_as=jnp.bfloat16):
    drawn = jax.random.normal(stream_key, shape, jnp.float32) * scale
    if len(shards) > 0:
        drawn = block_levels(stream_key, shape, shards, -0.22, 0.18) * drawn
    return jnp.clip(drawn, min=-most, max=most).astype(held_as)


def setup_inputs(seed: int = 0) -> dict:
    streams_of = jax.random.split(jax.random.key(seed), 17)
    tokens = noise(streams_of[0], (TOKENS, D), 1.0, 6.0, ((0, 128),))
    segments = jnp.searchsorted(jnp.cumsum(ragged(streams_of[1], REQS, TOKENS, TOK_ROW, 2)), jnp.arange(TOKENS), side="right").astype(jnp.int32)
    group_ids = plant(ranked_ids(streams_of[2], (REQS,), GROUPS, 2), jax.random.fold_in(streams_of[2], 3), 0, GROUPS - 1).astype(jnp.int32)
    prefix_owner = jax.random.permutation(streams_of[3], GROUPS).astype(jnp.int32)
    slab_fill = plant(jax.random.randint(streams_of[4], (GROUPS,), PREFIX // 2, PREFIX + 1), jax.random.fold_in(streams_of[4], 1), PREFIX // 2, PREFIX).astype(jnp.int32)
    prefix_cache = draw_prefix_cache(jax.random.fold_in(streams_of[16], 71), 0)
    attn_gain = jnp.clip(1.0 + 0.1 * jax.random.normal(streams_of[6], (D,), jnp.float32), 0.5, 1.5)
    w_query = noise(streams_of[7], (D, HQ * HS), D ** -0.5, 0.15625, ((1, 8),))
    w_keyval = noise(streams_of[8], (D, KVH * 2 * HS), D ** -0.5, 0.15625, ((1, 8),))
    w_out = noise(streams_of[9], (HQ * HS, D), (HQ * HS) ** -0.5, 0.15625, ((0, 8),))
    ffn_gain = jnp.clip(1.0 + 0.1 * jax.random.normal(streams_of[10], (D,), jnp.float32), 0.5, 1.5)
    routes_keys = jax.random.split(jax.random.fold_in(streams_of[11], 1), TOKENS // TOK_DEV)
    routes_turns = jax.random.permutation(jax.random.fold_in(streams_of[11], 3), TOKENS // TOK_DEV)
    routes = jax.vmap(lambda own, number: shared_out(jax.random.fold_in(streams_of[11], 2), own, number, TOK_DEV, EXPERTS, TOPK, CAP, 2))(routes_keys, routes_turns).reshape((TOKENS, TOPK))
    route_gates = jnp.clip(jnp.exp(math.log(0.5) - 2.3025851 * jax.random.uniform(streams_of[12], (TOKENS, TOPK), jnp.float32) ** block_levels(streams_of[12], (TOKENS, TOPK), ((0, 128),), -0.2, 0.2)), 0.05, 0.5)
    w_gate = noise(streams_of[13], (EXPERTS, D, FF), D ** -0.5, 0.15625, ((0, 16),))
    w_up = noise(streams_of[14], (EXPERTS, D, FF), D ** -0.5, 0.15625, ((0, 16),))
    w_down = noise(streams_of[15], (EXPERTS, FF, D), FF ** -0.5, 0.25, ((0, 16),))
    return dict(tokens=tokens, segments=segments, group_ids=group_ids, prefix_owner=prefix_owner, slab_fill=slab_fill, prefix_cache=prefix_cache, attn_gain=attn_gain, w_query=w_query, w_keyval=w_keyval, w_out=w_out, ffn_gain=ffn_gain, routes=routes, route_gates=route_gates, w_gate=w_gate, w_up=w_up, w_down=w_down)


NEG_FILL = -1e+30
NORM_EPS = 1e-06

def rms_scale(values, gain):
    widened = values.astype(jnp.float32)
    spread = lax.optimization_barrier(jnp.mean(widened * widened, axis=-1, keepdims=True))
    return widened * lax.rsqrt(spread + NORM_EPS) * gain

def lookup(table, index):
    entries = jnp.arange(table.shape[0], dtype=jnp.int32)
    return lax.optimization_barrier(jnp.sum(jnp.where(index[..., None] == entries, table, 0), axis=-1)).astype(jnp.int32)

def token_tables(segments, group_ids, prefix_owner, slab_fill):
    length_all = segments.shape[0]
    places = jnp.arange(length_all, dtype=jnp.int32)
    opening = jnp.concatenate([jnp.ones((1,), dtype=bool), segments[1:] != segments[:-1]])
    begins = lax.cummax(jnp.where(opening, places, 0), axis=0)
    slab_ids = lookup(prefix_owner, lookup(group_ids, segments))
    token_fill = lookup(slab_fill, slab_ids)
    return (slab_ids, token_fill, token_fill + places - begins)

def rope_angles(positions, head_size):
    steps_idx = jnp.arange(head_size // 2, dtype=jnp.float32)
    inverse = jnp.exp(steps_idx * (-2.0 * jnp.log(10000.0) / head_size))
    return positions.astype(jnp.float32)[:, None] * inverse[None, :]

def rotate(values, angles):
    halfway = values.shape[-1] // 2
    leading = values[..., :halfway]
    trailing = values[..., halfway:]
    cosine = jnp.cos(angles)[:, None, :]
    sine_v = jnp.sin(angles)[:, None, :]
    return jnp.concatenate([leading * cosine - trailing * sine_v, trailing * cosine + leading * sine_v], axis=-1)

def reference(tokens, segments, group_ids, prefix_owner, slab_fill, prefix_cache, attn_gain, w_query, w_keyval, w_out, ffn_gain, routes, route_gates, w_gate, w_up, w_down):
    group_share = HQ // KVH
    score_scale = HS ** (-0.5)
    normed = rms_scale(tokens, attn_gain).astype(jnp.bfloat16)
    slab_ids, token_fill, positions = token_tables(segments, group_ids, prefix_owner, slab_fill)
    angles = rope_angles(positions, HS)
    queries = jnp.dot(normed, w_query, preferred_element_type=jnp.float32).reshape(TOKENS, HQ, HS)
    keyval = jnp.dot(normed, w_keyval, preferred_element_type=jnp.float32).reshape(TOKENS, KVH, 2, HS)
    queries = rotate(queries, angles).astype(jnp.bfloat16).reshape(TOKENS, KVH, group_share, HS)
    keys_now = rotate(keyval[:, :, 0], angles).astype(jnp.bfloat16)
    values_now = keyval[:, :, 1].astype(jnp.bfloat16)
    cache_all = prefix_cache.reshape(GROUPS, PREFIX, KVH, 2, HS)
    window = TOK_ROW
    block_rows = TOK_DEV // 2
    keys_pad = jnp.concatenate([jnp.zeros((window, KVH, HS), jnp.bfloat16), keys_now], axis=0)
    values_pad = jnp.concatenate([jnp.zeros((window, KVH, HS), jnp.bfloat16), values_now], axis=0)
    segs_pad = jnp.concatenate([jnp.full((window,), -1, jnp.int32), segments], axis=0)

    def attend(first_row):
        first_row = first_row.astype(jnp.int32)
        query_blk = lax.dynamic_slice_in_dim(queries, first_row, block_rows, 0).astype(jnp.float32)
        query_seg = lax.dynamic_slice_in_dim(segments, first_row, block_rows, 0)
        query_pos = first_row + jnp.arange(block_rows, dtype=jnp.int32)
        query_slab = lax.dynamic_slice_in_dim(slab_ids, first_row, block_rows, 0)
        query_fill = lax.dynamic_slice_in_dim(token_fill, first_row, block_rows, 0)
        near_keys = lax.dynamic_slice_in_dim(keys_pad, first_row, window + block_rows, 0).astype(jnp.float32)
        near_vals = lax.dynamic_slice_in_dim(values_pad, first_row, window + block_rows, 0).astype(jnp.float32)
        near_segs = lax.dynamic_slice_in_dim(segs_pad, first_row, window + block_rows, 0)
        near_pos = first_row - window + jnp.arange(window + block_rows, dtype=jnp.int32)
        prefix_rows = cache_all[query_slab]
        prefix_keys = prefix_rows[:, :, :, 0].astype(jnp.float32)
        prefix_vals = prefix_rows[:, :, :, 1].astype(jnp.float32)
        far_scores = jnp.einsum('qgrd,qkgd->qgrk', query_blk, prefix_keys) * score_scale
        near_scores = jnp.einsum('qgrd,kgd->qgrk', query_blk, near_keys) * score_scale
        far_mask = (jnp.arange(PREFIX, dtype=jnp.int32)[None, :] < query_fill[:, None])[:, None, None, :]
        near_mask = ((near_segs[None, :] == query_seg[:, None]) & (near_pos[None, :] <= query_pos[:, None]))[:, None, None, :]
        far_scores = jnp.where(far_mask, far_scores, NEG_FILL)
        near_scores = jnp.where(near_mask, near_scores, NEG_FILL)
        peak_score = jnp.maximum(lax.optimization_barrier(jnp.max(far_scores, axis=-1)), lax.optimization_barrier(jnp.max(near_scores, axis=-1)))
        far_weights = jnp.where(far_mask, jnp.exp(far_scores - peak_score[..., None]), 0.0)
        near_weights = jnp.where(near_mask, jnp.exp(near_scores - peak_score[..., None]), 0.0)
        weight_sum = lax.optimization_barrier(jnp.sum(far_weights, axis=-1)) + lax.optimization_barrier(jnp.sum(near_weights, axis=-1))
        far_round = lax.optimization_barrier(far_weights.astype(jnp.bfloat16)).astype(jnp.float32)
        near_round = lax.optimization_barrier(near_weights.astype(jnp.bfloat16)).astype(jnp.float32)
        mixed_blk = jnp.einsum('qgrk,qkgd->qgrd', far_round, prefix_vals) + jnp.einsum('qgrk,kgd->qgrd', near_round, near_vals)
        mixed_blk = mixed_blk / weight_sum[..., None]
        return mixed_blk.reshape(block_rows, HQ * HS).astype(jnp.bfloat16)
    starts_all = jnp.arange(TOKENS // block_rows, dtype=jnp.int32) * block_rows
    mixed = lax.map(attend, starts_all).reshape(TOKENS, HQ * HS)
    hidden = tokens.astype(jnp.float32) + jnp.dot(mixed, w_out, preferred_element_type=jnp.float32)
    expert_in = rms_scale(hidden, ffn_gain).astype(jnp.bfloat16)
    capacity_rows = TOKENS // TOK_DEV * CAP

    def run_expert(summed, expert):
        chosen = routes == expert
        is_used = jnp.any(chosen, axis=1)
        weight_of = lax.optimization_barrier(jnp.sum(jnp.where(chosen, route_gates, 0.0), axis=1))
        picked = jnp.nonzero(is_used, size=capacity_rows, fill_value=0)[0].astype(jnp.int32)
        is_valid = jnp.arange(capacity_rows, dtype=jnp.int32) < jnp.sum(is_used.astype(jnp.int32))
        rows_in = expert_in[picked]
        gate_val = jnp.dot(rows_in, w_gate[expert], preferred_element_type=jnp.float32)
        up_val = jnp.dot(rows_in, w_up[expert], preferred_element_type=jnp.float32)
        inner_act = (jax.nn.silu(gate_val) * up_val).astype(jnp.bfloat16)
        result = jnp.dot(inner_act, w_down[expert], preferred_element_type=jnp.float32).astype(jnp.bfloat16)
        weighted = jnp.where(is_valid[:, None], result.astype(jnp.float32) * weight_of[picked][:, None], 0.0)
        return (summed.at[picked].add(weighted), None)
    summed, _ = lax.scan(run_expert, jnp.zeros((TOKENS, D), jnp.float32), jnp.arange(EXPERTS, dtype=jnp.int32))
    return (hidden + summed).astype(jnp.bfloat16)
```

```python
import functools

import jax
import jax.numpy as jnp
from jax import lax
from jax.experimental import pallas as pl
from jax.experimental.pallas import tpu as pltpu
from jax.sharding import PartitionSpec as P

HS = 64
EXPERTS = 32
TOPK = 8
PREFIX = 512
NEG_FILL = -1e30
NORM_EPS = 1e-06
LOG2E = 1.4426950408889634
BF = jnp.bfloat16
F32 = jnp.float32
VMEM_CAP = 60 * 1024 * 1024


def rms_scale(values, gain):
    widened = values.astype(F32)
    spread = jnp.mean(widened * widened, axis=-1, keepdims=True)
    return widened * lax.rsqrt(spread + NORM_EPS) * gain


def request_tables(window, own, group_ids, prefix_owner, slab_fill):
    reqs = group_ids.shape[0]
    ids = jnp.arange(reqs, dtype=jnp.int32)
    slabs = jnp.arange(prefix_owner.shape[0], dtype=jnp.int32)
    begins = jnp.sum((window[None, :] < ids[:, None]).astype(jnp.int32), axis=1)
    slab_of = jnp.sum(jnp.where(group_ids[:, None] == slabs, prefix_owner, 0), axis=1)
    fill_of = jnp.sum(jnp.where(slab_of[:, None] == slabs, slab_fill, 0), axis=1)
    packed = (begins * 16 + slab_of) * 1024 + fill_of
    mine = jnp.sum(jnp.where(own[None, :] == ids[:, None], packed[:, None], 0), axis=0)
    return mine // (16 * 1024), (mine // 1024) % 16, mine % 1024


def project_kernel(x_ref, wq_ref, wkv_ref, cos_ref, sin_ref, q_ref, kv_ref):
    x = x_ref[...]
    heads = wq_ref.shape[1] // HS
    pq = jnp.dot(x, wq_ref[...], preferred_element_type=F32)
    pkv = jnp.dot(x, wkv_ref[...], preferred_element_type=F32)
    both = jnp.concatenate([pq, pkv], axis=1)
    width = both.shape[1]
    lane = lax.broadcasted_iota(jnp.int32, both.shape, 1)
    swapped = jnp.where(
        lane % HS < HS // 2,
        pltpu.roll(both, width - HS // 2, 1),
        pltpu.roll(both, HS // 2, 1),
    )
    copies = -(-width // 128)
    cos = jnp.concatenate([cos_ref[...]] * copies, axis=1)[:, :width]
    sin = jnp.concatenate([sin_ref[...]] * copies, axis=1)[:, :width]
    turned = jnp.where(lane < (heads + 1) * HS, both * cos + swapped * sin, both).astype(BF)
    pad = jnp.zeros((x.shape[0], HS), BF)
    for head in range(heads):
        q_ref[head] = jnp.concatenate([turned[:, head * HS : (head + 1) * HS], pad], axis=1)
    kv_ref[...] = turned[:, heads * HS :]


def project(x, w_query, w_keyval, cos, sin, rows=256):
    length = x.shape[0]
    heads = w_query.shape[1] // HS
    whole = lambda a: pl.BlockSpec(a.shape, lambda i: (0,) * a.ndim)
    return pl.pallas_call(
        project_kernel,
        grid=(length // rows,),
        in_specs=[
            pl.BlockSpec((rows, x.shape[1]), lambda i: (i, 0)),
            whole(w_query),
            whole(w_keyval),
            pl.BlockSpec((rows, 128), lambda i: (i, 0)),
            pl.BlockSpec((rows, 128), lambda i: (i, 0)),
        ],
        out_specs=[
            pl.BlockSpec((heads, rows, 128), lambda i: (0, i, 0)),
            pl.BlockSpec((rows, 128), lambda i: (i, 0)),
        ],
        out_shape=[
            jax.ShapeDtypeStruct((heads, length, 128), BF),
            jax.ShapeDtypeStruct((length, 128), BF),
        ],
        compiler_params=pltpu.CompilerParams(vmem_limit_bytes=VMEM_CAP),
        name="project",
    )(x, w_query, w_keyval, cos, sin)


def attend_kernel(
    steps_ref, used_ref, fill_ref, q_ref, prev_ref, now_ref, cache_ref, rows_ref, wout_ref, out_ref, near_ref
):
    block = pl.program_id(0)
    heads, span = q_ref.shape[0], q_ref.shape[1]
    row_len = now_ref.shape[0]
    scale = HS ** (-0.5) * LOG2E

    @pl.when(block == 0)
    def _():
        near_ref[:row_len] = prev_ref[...]
        near_ref[row_len:] = now_ref[...]

    queries = jnp.concatenate([q_ref[h] for h in range(heads)], axis=0)
    begins = jnp.concatenate([rows_ref[0:1]] * heads, axis=1)
    slabs = jnp.concatenate([rows_ref[1:2]] * heads, axis=1)
    offset = row_len + block * span
    wide = heads * span

    def scores(kv):
        return lax.dot_general(kv, queries, (((1,), (1,)), ((), ())), preferred_element_type=F32)

    def absorb(s, kv, carry):
        peak, total, acc = carry
        peak_new = jnp.maximum(peak, jnp.max(s, axis=0, keepdims=True))
        factor = jnp.exp2((peak - peak_new) * scale)
        weights = jnp.exp2((s - peak_new) * scale)
        total = total * factor + jnp.sum(weights, axis=0, keepdims=True)
        values = kv.T[HS:]
        acc = acc * factor + jnp.dot(values, weights.astype(BF), preferred_element_type=F32)
        return peak_new, total, acc

    kv = near_ref[pl.ds(pl.multiple_of(offset, span), span)]
    key = lax.broadcasted_iota(jnp.int32, (span, wide), 0)
    query = lax.broadcasted_iota(jnp.int32, (span, wide), 1) % span
    s = jnp.where((key <= query) & (key >= begins - offset), scores(kv), NEG_FILL)
    carry = (
        jnp.full((1, wide), NEG_FILL, F32),
        jnp.zeros((1, wide), F32),
        jnp.zeros((HS, wide), F32),
    )
    carry = absorb(s, kv, carry)

    chunk = 2 * span

    def near_step(step, carry):
        first = pl.multiple_of(offset - (step + 1) * chunk, span)
        kv = near_ref[pl.ds(first, chunk)]
        key = lax.broadcasted_iota(jnp.int32, (chunk, wide), 0)
        s = jnp.where(key >= begins - first, scores(kv), NEG_FILL)
        return absorb(s, kv, carry)

    carry = lax.fori_loop(0, steps_ref[block], near_step, carry)

    def far_step(step, carry):
        slab = used_ref[block, step + 1]
        kv = cache_ref[pl.ds(pl.multiple_of(slab * PREFIX, PREFIX), PREFIX)]
        key = lax.broadcasted_iota(jnp.int32, (PREFIX, wide), 0)
        limit = jnp.where(slabs == slab, fill_ref[slab], 0)
        s = jnp.where(key < limit, scores(kv), NEG_FILL)
        return absorb(s, kv, carry)

    _, total, acc = lax.fori_loop(0, used_ref[block, 0], far_step, carry)
    mixed = (acc / total).T
    mixed = jnp.concatenate([mixed[h * span : (h + 1) * span] for h in range(heads)], axis=1)
    out_ref[...] = jnp.dot(mixed.astype(BF), wout_ref[...], preferred_element_type=F32).astype(BF)


def attend(q, kv_prev, kv_now, cache, rows, steps, used, fill, w_out, span=128):
    heads, length, _ = q.shape
    whole = lambda a: pl.BlockSpec(a.shape, lambda i, *_: (0,) * a.ndim)
    return pl.pallas_call(
        attend_kernel,
        grid_spec=pltpu.PrefetchScalarGridSpec(
            num_scalar_prefetch=3,
            grid=(length // span,),
            in_specs=[
                pl.BlockSpec((heads, span, 128), lambda i, *_: (0, i, 0)),
                whole(kv_prev),
                whole(kv_now),
                whole(cache),
                pl.BlockSpec((8, span), lambda i, *_: (0, i)),
                whole(w_out),
            ],
            out_specs=pl.BlockSpec((span, w_out.shape[1]), lambda i, *_: (i, 0)),
            scratch_shapes=[pltpu.VMEM((2 * length, 128), BF)],
        ),
        out_shape=jax.ShapeDtypeStruct((length, w_out.shape[1]), BF),
        compiler_params=pltpu.CompilerParams(vmem_limit_bytes=VMEM_CAP),
        name="attend",
    )(steps, used, fill, q, kv_prev, kv_now, cache, rows, w_out)


def expert_kernel(first_ref, x_ref, gates_ref, wg_ref, wu_ref, wd_ref, out_ref):
    x = x_ref[...]
    gates = gates_ref[...]
    lane = lax.broadcasted_iota(jnp.int32, gates.shape, 1)
    total = jnp.zeros((x.shape[0], wd_ref.shape[2]), F32)
    for e in range(wg_ref.shape[0]):
        gate = jnp.sum(jnp.where(lane == first_ref[0] + e, gates, 0.0), axis=1, keepdims=True)
        g = jnp.dot(x, wg_ref[e], preferred_element_type=F32)
        u = jnp.dot(x, wu_ref[e], preferred_element_type=F32)
        act = (g / (1.0 + jnp.exp(-g)) * u).astype(BF)
        o = jnp.dot(act, wd_ref[e], preferred_element_type=F32).astype(BF).astype(F32)
        total = total + gate * o
    out_ref[...] = total.astype(BF)


def run_experts(first, x, gates, w_gate, w_up, w_down, rows=256):
    length, width = x.shape
    whole = lambda a: pl.BlockSpec(a.shape, lambda i, *_: (0,) * a.ndim, pipeline_mode=pl.Buffered(1))
    return pl.pallas_call(
        expert_kernel,
        grid_spec=pltpu.PrefetchScalarGridSpec(
            num_scalar_prefetch=1,
            grid=(length // rows,),
            in_specs=[
                pl.BlockSpec((rows, width), lambda i, *_: (i, 0)),
                pl.BlockSpec((rows, gates.shape[1]), lambda i, *_: (i, 0)),
                whole(w_gate),
                whole(w_up),
                whole(w_down),
            ],
            out_specs=pl.BlockSpec((rows, width), lambda i, *_: (i, 0)),
        ),
        out_shape=jax.ShapeDtypeStruct((length, width), BF),
        compiler_params=pltpu.CompilerParams(vmem_limit_bytes=VMEM_CAP),
        name="experts",
    )(first, x, gates, w_gate, w_up, w_down)


def local(
    tokens,
    segments,
    group_ids,
    prefix_owner,
    slab_fill,
    prefix_cache,
    attn_gain,
    w_query,
    w_keyval,
    w_out,
    ffn_gain,
    routes,
    route_gates,
    w_gate,
    w_up,
    w_down,
):
    tok_count = lax.axis_size("tok")
    head_count = lax.axis_size("head")
    place = lax.axis_index("tok")
    row_len = tokens.shape[0] * head_count
    normed = rms_scale(tokens, attn_gain).astype(BF)
    gathered = lax.all_gather(normed, "head", axis=0, tiled=True)
    cache = lax.all_gather(prefix_cache, "tok", axis=0, tiled=True)

    padded = jnp.concatenate([jnp.full((row_len,), -1, jnp.int32), segments])
    window = lax.dynamic_slice_in_dim(padded, place * row_len, 2 * row_len, 0)
    own = window[row_len:]
    begins, slabs, fills = request_tables(window, own, group_ids, prefix_owner, slab_fill)
    positions = fills + row_len + jnp.arange(row_len, dtype=jnp.int32) - begins
    lane = jnp.arange(128, dtype=jnp.int32)
    steps_idx = (lane % (HS // 2)).astype(F32)
    inverse = jnp.exp(steps_idx * (-2.0 * jnp.log(10000.0) / HS))
    angles = positions.astype(F32)[:, None] * inverse[None, :]
    cos = jnp.cos(angles)
    sin = jnp.where(lane % HS < HS // 2, -jnp.sin(angles), jnp.sin(angles))

    span = 128
    blocks = row_len // span
    first_begin = begins.reshape(blocks, span)[:, 0]
    ends = row_len + jnp.arange(blocks, dtype=jnp.int32) * span
    steps = jnp.maximum(ends - first_begin + 2 * span - 1, 0) // (2 * span)
    ids = jnp.arange(tok_count, dtype=jnp.int32)
    present = jnp.max((slabs.reshape(blocks, span)[:, :, None] == ids).astype(jnp.int32), axis=1)
    earlier = jnp.sum(jnp.where(ids[:, None] < ids[None, :], present[:, :, None], 0), axis=1)
    listed = (present[:, None, :] == 1) & (earlier[:, None, :] == ids[None, :, None])
    used = jnp.sum(jnp.where(listed, ids, 0), axis=2)
    used = jnp.concatenate([jnp.sum(present, axis=1, keepdims=True), used], axis=1)
    rows = jnp.concatenate([begins[None], slabs[None], jnp.zeros((6, row_len), jnp.int32)], axis=0)

    q, kv_now = project(gathered, w_query, w_keyval, cos, sin)
    kv_prev = lax.ppermute(kv_now, "tok", [(i, i + 1) for i in range(tok_count - 1)])
    partial = attend(q, kv_prev, kv_now, cache, rows, steps, used, slab_fill, w_out)
    attended = lax.psum_scatter(partial, "head", scatter_dimension=0, tiled=True).astype(F32)
    hidden = tokens.astype(F32) + attended
    expert_in = rms_scale(hidden, ffn_gain).astype(BF)

    experts = jnp.arange(EXPERTS, dtype=jnp.int32)
    gates = jnp.sum(jnp.where(routes[:, :, None] == experts, route_gates[:, :, None], 0.0), axis=1)
    gates_all = lax.all_gather(gates, "tok", axis=0, tiled=True)
    arrived = lax.all_gather(expert_in, "tok", axis=0, tiled=True)
    first = (place * w_gate.shape[0]).astype(jnp.int32).reshape(1)
    answered = run_experts(first, arrived, gates_all, w_gate, w_up, w_down)
    mixture = lax.psum_scatter(answered, "tok", scatter_dimension=0, tiled=True)
    return (hidden + mixture.astype(F32)).astype(BF)


def solution(mesh):
    return jax.shard_map(
        local,
        mesh=mesh,
        in_specs=(
            P(("tok", "head"), None),
            P(),
            P(),
            P(),
            P(),
            P("tok", "head"),
            P(),
            P(None, "head"),
            P(None, "head"),
            P("head", None),
            P(),
            P(("tok", "head"), None),
            P(("tok", "head"), None),
            P("tok", None, None),
            P("tok", None, None),
            P("tok", None, None),
        ),
        out_specs=P(("tok", "head"), None),
        check_vma=False,
    )
```

```python
import functools

import jax
import jax.numpy as jnp
from jax import lax
from jax.experimental import pallas as pl
from jax.experimental.pallas import tpu as pltpu
from jax.sharding import PartitionSpec as P

HS = 64
EXPERTS = 32
TOPK = 8
PREFIX = 512
NEG_FILL = -1e30
NORM_EPS = 1e-06
LOG2E = 1.4426950408889634
BF = jnp.bfloat16
F32 = jnp.float32
VMEM_CAP = 60 * 1024 * 1024


def rms_scale(values, gain):
    widened = values.astype(F32)
    spread = jnp.mean(widened * widened, axis=-1, keepdims=True)
    return widened * lax.rsqrt(spread + NORM_EPS) * gain


def request_tables(window, own, group_ids, prefix_owner, slab_fill):
    reqs = group_ids.shape[0]
    ids = jnp.arange(reqs, dtype=jnp.int32)
    slabs = jnp.arange(prefix_owner.shape[0], dtype=jnp.int32)
    begins = jnp.sum((window[None, :] < ids[:, None]).astype(jnp.int32), axis=1)
    slab_of = jnp.sum(jnp.where(group_ids[:, None] == slabs, prefix_owner, 0), axis=1)
    fill_of = jnp.sum(jnp.where(slab_of[:, None] == slabs, slab_fill, 0), axis=1)
    packed = (begins * 16 + slab_of) * 1024 + fill_of
    mine = jnp.sum(jnp.where(own[None, :] == ids[:, None], packed[:, None], 0), axis=0)
    return mine // (16 * 1024), (mine // 1024) % 16, mine % 1024


def project_kernel(x_ref, wq_ref, wkv_ref, cos_ref, sin_ref, q_ref, kv_ref):
    x = x_ref[...]
    heads = wq_ref.shape[1] // HS
    pq = jnp.dot(x, wq_ref[...], preferred_element_type=F32)
    pkv = jnp.dot(x, wkv_ref[...], preferred_element_type=F32)
    both = jnp.concatenate([pq, pkv], axis=1)
    width = both.shape[1]
    lane = lax.broadcasted_iota(jnp.int32, both.shape, 1)
    swapped = jnp.where(
        lane % HS < HS // 2,
        pltpu.roll(both, width - HS // 2, 1),
        pltpu.roll(both, HS // 2, 1),
    )
    copies = -(-width // 128)
    cos = jnp.concatenate([cos_ref[...]] * copies, axis=1)[:, :width]
    sin = jnp.concatenate([sin_ref[...]] * copies, axis=1)[:, :width]
    turned = jnp.where(lane < (heads + 1) * HS, both * cos + swapped * sin, both).astype(BF)
    pad = jnp.zeros((x.shape[0], HS), BF)
    for head in range(heads):
        q_ref[head] = jnp.concatenate([turned[:, head * HS : (head + 1) * HS], pad], axis=1)
    kv_ref[...] = turned[:, heads * HS :]


def project(x, w_query, w_keyval, cos, sin, rows=256):
    length = x.shape[0]
    heads = w_query.shape[1] // HS
    whole = lambda a: pl.BlockSpec(a.shape, lambda i: (0,) * a.ndim)
    return pl.pallas_call(
        project_kernel,
        grid=(length // rows,),
        in_specs=[
            pl.BlockSpec((rows, x.shape[1]), lambda i: (i, 0)),
            whole(w_query),
            whole(w_keyval),
            pl.BlockSpec((rows, 128), lambda i: (i, 0)),
            pl.BlockSpec((rows, 128), lambda i: (i, 0)),
        ],
        out_specs=[
            pl.BlockSpec((heads, rows, 128), lambda i: (0, i, 0)),
            pl.BlockSpec((rows, 128), lambda i: (i, 0)),
        ],
        out_shape=[
            jax.ShapeDtypeStruct((heads, length, 128), BF),
            jax.ShapeDtypeStruct((length, 128), BF),
        ],
        compiler_params=pltpu.CompilerParams(vmem_limit_bytes=VMEM_CAP),
        name="project",
    )(x, w_query, w_keyval, cos, sin)


def attend_kernel(
    steps_ref, used_ref, fill_ref, q_ref, prev_ref, now_ref, cache_ref, rows_ref, wout_ref, out_ref, near_ref
):
    block = pl.program_id(0)
    heads, span = q_ref.shape[0], q_ref.shape[1]
    row_len = now_ref.shape[0]
    scale = HS ** (-0.5) * LOG2E

    @pl.when(block == 0)
    def _():
        near_ref[:row_len] = prev_ref[...]
        near_ref[row_len:] = now_ref[...]

    queries = jnp.concatenate([q_ref[h] for h in range(heads)], axis=0)
    begins = jnp.concatenate([rows_ref[0:1]] * heads, axis=1)
    slabs = jnp.concatenate([rows_ref[1:2]] * heads, axis=1)
    offset = row_len + block * span
    wide = heads * span

    def scores(kv):
        return lax.dot_general(kv, queries, (((1,), (1,)), ((), ())), preferred_element_type=F32)

    def absorb(s, kv, carry):
        peak, total, acc = carry
        peak_new = jnp.maximum(peak, jnp.max(s, axis=0, keepdims=True))
        factor = jnp.exp2((peak - peak_new) * scale)
        weights = jnp.exp2((s - peak_new) * scale)
        total = total * factor + jnp.sum(weights, axis=0, keepdims=True)
        values = kv.T[HS:]
        acc = acc * factor + jnp.dot(values, weights.astype(BF), preferred_element_type=F32)
        return peak_new, total, acc

    kv = near_ref[pl.ds(pl.multiple_of(offset, span), span)]
    key = lax.broadcasted_iota(jnp.int32, (span, wide), 0)
    query = lax.broadcasted_iota(jnp.int32, (span, wide), 1) % span
    s = jnp.where((key <= query) & (key >= begins - offset), scores(kv), NEG_FILL)
    carry = (
        jnp.full((1, wide), NEG_FILL, F32),
        jnp.zeros((1, wide), F32),
        jnp.zeros((HS, wide), F32),
    )
    carry = absorb(s, kv, carry)

    chunk = 2 * span

    def near_step(step, carry):
        first = pl.multiple_of(offset - (step + 1) * chunk, span)
        kv = near_ref[pl.ds(first, chunk)]
        key = lax.broadcasted_iota(jnp.int32, (chunk, wide), 0)
        s = jnp.where(key >= begins - first, scores(kv), NEG_FILL)
        return absorb(s, kv, carry)

    carry = lax.fori_loop(0, steps_ref[block], near_step, carry)

    def far_step(step, carry):
        slab = used_ref[block, step + 1]
        kv = cache_ref[pl.ds(pl.multiple_of(slab * PREFIX, PREFIX), PREFIX)]
        key = lax.broadcasted_iota(jnp.int32, (PREFIX, wide), 0)
        limit = jnp.where(slabs == slab, fill_ref[slab], 0)
        s = jnp.where(key < limit, scores(kv), NEG_FILL)
        return absorb(s, kv, carry)

    _, total, acc = lax.fori_loop(0, used_ref[block, 0], far_step, carry)
    mixed = (acc / total).T
    mixed = jnp.concatenate([mixed[h * span : (h + 1) * span] for h in range(heads)], axis=1)
    out_ref[...] = jnp.dot(mixed.astype(BF), wout_ref[...], preferred_element_type=F32).astype(BF)


def attend(q, kv_prev, kv_now, cache, rows, steps, used, fill, w_out, span=128):
    heads, length, _ = q.shape
    whole = lambda a: pl.BlockSpec(a.shape, lambda i, *_: (0,) * a.ndim)
    return pl.pallas_call(
        attend_kernel,
        grid_spec=pltpu.PrefetchScalarGridSpec(
            num_scalar_prefetch=3,
            grid=(length // span,),
            in_specs=[
                pl.BlockSpec((heads, span, 128), lambda i, *_: (0, i, 0)),
                whole(kv_prev),
                whole(kv_now),
                whole(cache),
                pl.BlockSpec((8, span), lambda i, *_: (0, i)),
                whole(w_out),
            ],
            out_specs=pl.BlockSpec((span, w_out.shape[1]), lambda i, *_: (i, 0)),
            scratch_shapes=[pltpu.VMEM((2 * length, 128), BF)],
        ),
        out_shape=jax.ShapeDtypeStruct((length, w_out.shape[1]), BF),
        compiler_params=pltpu.CompilerParams(vmem_limit_bytes=VMEM_CAP),
        name="attend",
    )(steps, used, fill, q, kv_prev, kv_now, cache, rows, w_out)


def expert_kernel(x_ref, gates_ref, wg_ref, wu_ref, wd_ref, out_ref):
    x = x_ref[...]
    gates = jnp.concatenate([gates_ref[s].T for s in range(gates_ref.shape[0])], axis=0)
    total = jnp.zeros((x.shape[0], wd_ref.shape[2]), F32)
    for e in range(wg_ref.shape[0]):
        gate = gates[:, e : e + 1]
        g = jnp.dot(x, wg_ref[e], preferred_element_type=F32)
        u = jnp.dot(x, wu_ref[e], preferred_element_type=F32)
        act = (g / (1.0 + jnp.exp(-g)) * u).astype(BF)
        o = jnp.dot(act, wd_ref[e], preferred_element_type=F32).astype(BF).astype(F32)
        total = total + gate * o
    out_ref[...] = total.astype(BF)


def run_experts(x, gates, w_gate, w_up, w_down, rows=256):
    length, width = x.shape
    whole = lambda a: pl.BlockSpec(a.shape, lambda i: (0,) * a.ndim, pipeline_mode=pl.Buffered(1))
    return pl.pallas_call(
        expert_kernel,
        grid=(length // rows,),
        in_specs=[
            pl.BlockSpec((rows, width), lambda i: (i, 0)),
            pl.BlockSpec((rows // gates.shape[2],) + gates.shape[1:], lambda i: (i, 0, 0)),
            whole(w_gate),
            whole(w_up),
            whole(w_down),
        ],
        out_specs=pl.BlockSpec((rows, width), lambda i: (i, 0)),
        out_shape=jax.ShapeDtypeStruct((length, width), BF),
        compiler_params=pltpu.CompilerParams(vmem_limit_bytes=VMEM_CAP),
        name="experts",
    )(x, gates, w_gate, w_up, w_down)


MESH_ID = pl.DeviceIdType.MESH


def torus_messages():
    keys = []
    for half in (0, 1):
        for sign in (1, -1):
            keys.append(("near", half, 0, sign))
            keys.append(("far", half, 0, sign))
            for a in (0, -1, 1, 2):
                keys.append(("side", half, a, sign))
                keys.append(("last", half, a, sign))
    return {key: i for i, key in enumerate(keys)}


def place_of(place, dx, dy):
    return ((place // 4 + dx + 4) % 4) * 4 + (place % 4 + dy + 4) % 4


def torus_gather(own, out, rows, sends, receives, keys):
    place, head = lax.axis_index("tok"), lax.axis_index("head")
    half_rows, part = rows // 2, rows // 4
    started = []

    def unit(half, a, b):
        return (a, b) if half == 0 else (b, a)

    def copy(key, landing=False):
        kind, half, a, sign = key
        first = kind in ("near", "far")
        if kind == "near":
            source = (0, 0)
        elif kind == "far":
            source = (-sign, 0)
        elif kind == "side":
            source = (a, 0)
        else:
            source = (a, -sign)
        begin, size = half * half_rows, half_rows
        if kind in ("far", "last"):
            begin, size = begin + (0 if sign == 1 else part), part
        if landing:
            source = (source[0] - sign, source[1]) if first else (source[0], source[1] - sign)
        slot = place_of(place, *unit(half, *source))
        step = unit(half, sign, 0) if first else unit(half, 0, sign)
        target = out.at[slot, pl.ds(begin, size)]
        if not landing and source == (0, 0):
            src = own.at[pl.ds(begin, size)]
        else:
            src = target
        return pltpu.make_async_remote_copy(
            src_ref=src,
            dst_ref=target,
            send_sem=sends.at[keys[key]],
            recv_sem=receives.at[keys[key]],
            device_id=(place_of(place, *step), head),
            device_id_type=MESH_ID,
        )

    def send(*key):
        c = copy(key)
        c.start()
        started.append(c)

    def arrive(*key):
        copy(key, landing=True).wait_recv()

    for sign in (1, -1):
        for half in (0, 1):
            send("near", half, 0, sign)
    for sign in (1, -1):
        for half in (0, 1):
            send("side", half, 0, sign)
    yield
    for sign in (1, -1):
        for half in (0, 1):
            arrive("near", half, 0, sign)
            send("far", half, 0, sign)
            send("side", half, -sign, 1)
            send("side", half, -sign, -1)
    yield
    for sign in (1, -1):
        for half in (0, 1):
            arrive("side", half, 0, sign)
            send("last", half, 0, sign)
    yield
    for half in (0, 1):
        for sign in (1, -1):
            arrive("far", half, 0, sign)
        for sign in (1, -1):
            send("side", half, 2, sign)
    yield
    for a in (-1, 1, 2):
        for sign in (1, -1):
            for half in (0, 1):
                arrive("side", half, a, sign)
                send("last", half, a, sign)
        yield
    for a in (0, -1, 1, 2):
        for half in (0, 1):
            for sign in (1, -1):
                arrive("last", half, a, sign)
    for c in started:
        c.wait_send()
    yield


def greet(peers):
    barrier = pltpu.get_barrier_semaphore()
    for peer in peers:
        pl.semaphore_signal(barrier, inc=1, device_id=peer, device_id_type=MESH_ID)
    pl.semaphore_wait(barrier, len(peers))


def torus_peers():
    place, head = lax.axis_index("tok"), lax.axis_index("head")
    return [(place_of(place, *s), head) for s in ((1, 0), (-1, 0), (0, 1), (0, -1))]


def scatter_messages():
    keys = []
    for half in (0, 1):
        for a in (2, -1, 1, 0):
            for sign in (1, -1):
                for kind in ("far", "plain", "added"):
                    keys.append((kind, half, a, sign))
        for sign in (1, -1):
            for kind in ("far2", "plain2", "added2"):
                keys.append((kind, half, 0, sign))
    return {key: i for i, key in enumerate(keys)}


def torus_scatter(parts, land, rows, sends, receives, keys):
    place, head = lax.axis_index("tok"), lax.axis_index("head")
    half_rows, part = rows // 2, rows // 4
    started = []

    def unit(half, a, b):
        return (a, b) if half == 0 else (b, a)

    def spot(key):
        kind, half, a, sign = key
        second = kind.endswith("2")
        base = half * half_rows
        low, high = pl.ds(base, part), pl.ds(base + part, part)
        with_far, plain = (low, high) if sign == 1 else (high, low)
        distance = 2 if kind.startswith("far") else sign
        offset = (distance, 0) if second else (a, distance)
        rows_of = plain if kind.startswith("plain") else with_far
        return place_of(place, *unit(half, *offset)), rows_of

    def copy(key):
        kind, half, a, sign = key
        slot, rows_of = spot(key)
        step = unit(half, sign, 0) if kind.endswith("2") else unit(half, 0, sign)
        return pltpu.make_async_remote_copy(
            src_ref=parts.at[slot, rows_of],
            dst_ref=land.at[keys[key]],
            send_sem=sends.at[keys[key]],
            recv_sem=receives.at[keys[key]],
            device_id=(place_of(place, *step), head),
            device_id_type=MESH_ID,
        )

    def send(*key):
        c = copy(key)
        c.start()
        started.append(c)

    def add(key, slot, rows_of):
        copy(key).wait_recv()
        parts[slot, rows_of] = (
            parts[slot, rows_of].astype(F32) + land[keys[key]].astype(F32)
        ).astype(parts.dtype)

    order = (2, -1, 1, 0)
    for a in order:
        for sign in (1, -1):
            for half in (0, 1):
                send("far", half, a, sign)
        for sign in (1, -1):
            for half in (0, 1):
                send("plain", half, a, sign)
        yield
    for step in range(len(order) + 1):
        if step < len(order):
            a = order[step]
            for sign in (1, -1):
                for half in (0, 1):
                    slot, rows_of = spot(("added", half, a, sign))
                    add(("far", half, a, sign), slot, rows_of)
                    send("added", half, a, sign)
            yield
        if step > 0:
            a = order[step - 1]
            for half in (0, 1):
                slot = place_of(place, *unit(half, a, 0))
                for sign in (1, -1):
                    for kind in ("plain", "added"):
                        _, rows_of = spot((kind, half, a, sign))
                        add((kind, half, a, sign), slot, rows_of)
                if a == 2:
                    for sign in (1, -1):
                        send("far2", half, 0, sign)
                elif a != 0:
                    send("plain2", half, 0, a)
            yield
        if step == 3:
            for half in (0, 1):
                for sign in (1, -1):
                    slot, rows_of = spot(("added2", half, 0, sign))
                    add(("far2", half, 0, sign), slot, rows_of)
                    send("added2", half, 0, sign)
            yield
    for half in (0, 1):
        for sign in (1, -1):
            for kind in ("plain2", "added2"):
                _, rows_of = spot((kind, half, 0, sign))
                add((kind, half, 0, sign), place, rows_of)
    for c in started:
        c.wait_send()
    yield


def scatter_kernel(x_ref, hidden_ref, out_ref, parts, land, sends, receives, own_sems):
    keys = scatter_messages()
    loads = [pltpu.make_async_copy(x_ref.at[s], parts.at[s], own_sems.at[s]) for s in range(parts.shape[0])]
    for c in loads:
        c.start()
    greet(torus_peers())
    for c in loads:
        c.wait()
    for _ in torus_scatter(parts, land, parts.shape[1], sends, receives, keys):
        pass
    out_ref[...] = (hidden_ref[...] + parts[lax.axis_index("tok")].astype(F32)).astype(out_ref.dtype)


def scatter_tok(x, hidden, collective_id):
    count = len(scatter_messages())
    _, rows, width = x.shape
    return pl.pallas_call(
        scatter_kernel,
        in_specs=[pl.BlockSpec(memory_space=pl.ANY), pl.BlockSpec(memory_space=pltpu.VMEM)],
        out_specs=pl.BlockSpec(memory_space=pltpu.VMEM),
        out_shape=jax.ShapeDtypeStruct((rows, width), x.dtype),
        scratch_shapes=[
            pltpu.VMEM(x.shape, x.dtype),
            pltpu.VMEM((count, rows // 4, width), x.dtype),
            pltpu.SemaphoreType.DMA((count,)),
            pltpu.SemaphoreType.DMA((count,)),
            pltpu.SemaphoreType.DMA((16,)),
        ],
        compiler_params=pltpu.CompilerParams(
            collective_id=collective_id, has_side_effects=True, vmem_limit_bytes=VMEM_CAP
        ),
        name="scatter_tok",
    )(x, hidden)


def ring_messages(kinds):
    return {key: i for i, key in enumerate(kinds)}


GATHER_RING = ring_messages(
    [("near", 1), ("near", -1), ("far", 1), ("far", -1), ("pair", 0), ("pair", 1), ("pair", -1), ("half", 1), ("half", -1)]
)
SCATTER_RING = ring_messages(
    [("pair", 2), ("pair", 1), ("pair", -1), ("pair", 0)]
    + [(kind, sign) for kind in ("far", "plain", "added") for sign in (1, -1)]
)


def head_of(head, dz, flip=0):
    core = head % 2
    return ((head // 2 + dz + 4) % 4) * 2 + (core + flip) % 2


def ring_peers():
    place, head = lax.axis_index("tok"), lax.axis_index("head")
    return [(place, head_of(head, 1)), (place, head_of(head, -1)), (place, head_of(head, 0, 1))]


def ring_gather(own, out, rows, sends, receives, keys):
    place, head = lax.axis_index("tok"), lax.axis_index("head")
    started = []

    def copy(key, landing=False):
        kind, value = key
        begin, size = 0, rows
        if kind in ("far", "half"):
            size = rows // 2
            begin = 0 if value == 1 else size
        dz = {"near": 0, "far": -value, "pair": value, "half": 2}[kind]
        crossing = kind in ("pair", "half")
        if landing:
            slot = head_of(head, dz, 1) if crossing else head_of(head, dz - value)
        else:
            slot = head_of(head, dz)
        target = out.at[slot, pl.ds(begin, size)]
        src = own.at[pl.ds(begin, size)] if not landing and dz == 0 else target
        peer = head_of(head, 0, 1) if crossing else head_of(head, value)
        return pltpu.make_async_remote_copy(
            src_ref=src,
            dst_ref=target,
            send_sem=sends.at[keys[key]],
            recv_sem=receives.at[keys[key]],
            device_id=(place, peer),
            device_id_type=MESH_ID,
        )

    def send(*key):
        c = copy(key)
        c.start()
        started.append(c)

    def arrive(*key):
        copy(key, landing=True).wait_recv()

    send("near", 1)
    send("near", -1)
    send("pair", 0)
    yield
    for sign in (1, -1):
        arrive("near", sign)
        send("far", sign)
        send("pair", -sign)
    yield
    for sign in (1, -1):
        arrive("far", sign)
        send("half", sign)
    yield
    for dz in (0, 1, -1):
        arrive("pair", dz)
    for sign in (1, -1):
        arrive("half", sign)
    for c in started:
        c.wait_send()
    yield


def opening_kernel(x_ref, cache_ref, gates_ref, x_out, cache_out, gates_out, ts, tr, hs, hr, gs, gr, own_sems):
    place, head = lax.axis_index("tok"), lax.axis_index("head")
    count = gates_ref.shape[0]
    others = [((place + d) % count, head) for d in range(1, count)]
    greet(others + ring_peers())
    mine = [
        pltpu.make_async_copy(x_ref, x_out.at[head], own_sems.at[0]),
        pltpu.make_async_copy(cache_ref, cache_out.at[place], own_sems.at[1]),
        pltpu.make_async_copy(gates_ref.at[place], gates_out.at[place], own_sems.at[2]),
    ]
    one = ring_gather(x_ref, x_out, x_ref.shape[0], hs, hr, GATHER_RING)
    two = torus_gather(cache_ref, cache_out, cache_ref.shape[0], ts, tr, torus_messages())

    def gate_copy(d, landing=False):
        target = (place + d) % count
        slot = (place - d + count) % count if landing else place
        return pltpu.make_async_remote_copy(
            src_ref=gates_ref.at[target],
            dst_ref=gates_out.at[slot],
            send_sem=gs.at[d],
            recv_sem=gr.at[d],
            device_id=(target, head),
            device_id_type=MESH_ID,
        )

    next(one)
    next(two)
    for c in mine:
        c.start()
    for d in range(1, count):
        gate_copy(d).start()
    for _ in range(2):
        next(one)
        next(two)
    for _ in two:
        pass
    for _ in one:
        pass
    for d in range(1, count):
        gate_copy(d, True).wait_recv()
    for d in range(1, count):
        gate_copy(d).wait_send()
    for c in mine:
        c.wait()


def opening(x, cache, gates, collective_id):
    t, r, n = len(torus_messages()), len(GATHER_RING), gates.shape[0]
    dma = pltpu.SemaphoreType.DMA
    return pl.pallas_call(
        opening_kernel,
        in_specs=[pl.BlockSpec(memory_space=pltpu.VMEM)] * 3,
        out_specs=[pl.BlockSpec(memory_space=pl.ANY)] * 3,
        out_shape=[
            jax.ShapeDtypeStruct((8,) + x.shape, x.dtype),
            jax.ShapeDtypeStruct((n,) + cache.shape, cache.dtype),
            jax.ShapeDtypeStruct(gates.shape, gates.dtype),
        ],
        scratch_shapes=[dma((t,)), dma((t,)), dma((r,)), dma((r,)), dma((n,)), dma((n,)), dma((3,))],
        compiler_params=pltpu.CompilerParams(collective_id=collective_id, has_side_effects=True),
        name="opening",
    )(x, cache, gates)


def ring_scatter(parts, pair_land, land, rows, sends, receives, keys):
    place, head = lax.axis_index("tok"), lax.axis_index("head")
    started = []
    low, high = pl.ds(0, rows // 2), pl.ds(rows // 2, rows // 2)

    def spot(key):
        kind, value = key
        if kind == "far":
            return head_of(head, 2), (low if value == 1 else high)
        if kind == "plain":
            return head_of(head, value), (high if value == 1 else low)
        return head_of(head, value), (low if value == 1 else high)

    def copy(key):
        kind, value = key
        if kind == "pair":
            src, dst = parts.at[head_of(head, value, 1)], pair_land.at[keys[key]]
            peer = head_of(head, 0, 1)
        else:
            slot, rows_of = spot(key)
            src, dst = parts.at[slot, rows_of], land.at[keys[key] - 4]
            peer = head_of(head, value)
        return pltpu.make_async_remote_copy(
            src_ref=src,
            dst_ref=dst,
            send_sem=sends.at[keys[key]],
            recv_sem=receives.at[keys[key]],
            device_id=(place, peer),
            device_id_type=MESH_ID,
        )

    def send(*key):
        c = copy(key)
        c.start()
        started.append(c)

    def add(key, slot, rows_of, buffer, index):
        copy(key).wait_recv()
        parts[slot, rows_of] = (parts[slot, rows_of].astype(F32) + buffer[index].astype(F32)).astype(parts.dtype)

    def add_pair(dz):
        key = ("pair", dz)
        add(key, head_of(head, dz), pl.ds(0, rows), pair_land, keys[key])

    for dz in (2, 1, -1, 0):
        send("pair", dz)
    add_pair(2)
    for sign in (1, -1):
        send("far", sign)
    for sign in (1, -1):
        add_pair(sign)
        send("plain", sign)
    add_pair(0)
    for sign in (1, -1):
        key = ("far", sign)
        slot, rows_of = spot(("added", sign))
        add(key, slot, rows_of, land, keys[key] - 4)
        send("added", sign)
    for kind in ("plain", "added"):
        for sign in (1, -1):
            key = (kind, sign)
            _, rows_of = spot(key)
            add(key, head, rows_of, land, keys[key] - 4)
    for c in started:
        c.wait_send()


def settle_kernel(
    part_ref, tokens_ref, gain_ref, hidden_ref, out_ref, parts, pair_land, land, normed, rs, rr, ts, tr, own_sems
):
    place, head = lax.axis_index("tok"), lax.axis_index("head")
    rows = tokens_ref.shape[0]
    loads = [
        pltpu.make_async_copy(part_ref.at[pl.ds(h * rows, rows)], parts.at[h], own_sems.at[h]) for h in range(8)
    ]
    for c in loads:
        c.start()
    greet(torus_peers() + ring_peers())
    for c in loads:
        c.wait()
    ring_scatter(parts, pair_land, land, rows, rs, rr, SCATTER_RING)
    hidden = tokens_ref[...].astype(F32) + parts[head].astype(F32)
    hidden_ref[...] = hidden
    normed[...] = rms_scale(hidden, gain_ref[...]).astype(normed.dtype)
    mine = pltpu.make_async_copy(normed, out_ref.at[place], own_sems.at[8])
    mine.start()
    for _ in torus_gather(normed, out_ref, rows, ts, tr, torus_messages()):
        pass
    mine.wait()


def settle(partial, tokens, gain, collective_id):
    rows, width = tokens.shape
    t, r = len(torus_messages()), len(SCATTER_RING)
    dma = pltpu.SemaphoreType.DMA
    return pl.pallas_call(
        settle_kernel,
        in_specs=[
            pl.BlockSpec(memory_space=pl.ANY),
            pl.BlockSpec(memory_space=pltpu.VMEM),
            pl.BlockSpec(memory_space=pltpu.VMEM),
        ],
        out_specs=[pl.BlockSpec(memory_space=pltpu.VMEM), pl.BlockSpec(memory_space=pl.ANY)],
        out_shape=[
            jax.ShapeDtypeStruct((rows, width), F32),
            jax.ShapeDtypeStruct((16, rows, width), BF),
        ],
        scratch_shapes=[
            pltpu.VMEM((8, rows, width), BF),
            pltpu.VMEM((4, rows, width), BF),
            pltpu.VMEM((6, rows // 2, width), BF),
            pltpu.VMEM((rows, width), BF),
            dma((r,)),
            dma((r,)),
            dma((t,)),
            dma((t,)),
            dma((9,)),
        ],
        compiler_params=pltpu.CompilerParams(
            collective_id=collective_id, has_side_effects=True, vmem_limit_bytes=VMEM_CAP
        ),
        name="settle",
    )(partial, tokens, gain)


def local(
    tokens,
    segments,
    group_ids,
    prefix_owner,
    slab_fill,
    prefix_cache,
    attn_gain,
    w_query,
    w_keyval,
    w_out,
    ffn_gain,
    routes,
    route_gates,
    w_gate,
    w_up,
    w_down,
):
    tok_count = lax.axis_size("tok")
    head_count = lax.axis_size("head")
    place = lax.axis_index("tok")
    row_len = tokens.shape[0] * head_count
    normed = rms_scale(tokens, attn_gain).astype(BF)
    exp_local = w_gate.shape[0]
    experts = jnp.arange(EXPERTS, dtype=jnp.int32)[:, None, None]
    gates = jnp.sum(jnp.where(routes.T[None] == experts, route_gates.T[None], 0.0), axis=1)
    gates = gates.reshape(tok_count, exp_local, -1)
    gates = jnp.concatenate([gates, jnp.zeros((tok_count, 8 - exp_local, gates.shape[2]), F32)], axis=1)
    gathered, cache, gates_all = opening(normed, prefix_cache, gates, 1)
    gathered = gathered.reshape(row_len, -1)
    cache = cache.reshape(-1, cache.shape[-1])

    padded = jnp.concatenate([jnp.full((row_len,), -1, jnp.int32), segments])
    window = lax.dynamic_slice_in_dim(padded, place * row_len, 2 * row_len, 0)
    own = window[row_len:]
    begins, slabs, fills = request_tables(window, own, group_ids, prefix_owner, slab_fill)
    positions = fills + row_len + jnp.arange(row_len, dtype=jnp.int32) - begins
    lane = jnp.arange(128, dtype=jnp.int32)
    steps_idx = (lane % (HS // 2)).astype(F32)
    inverse = jnp.exp(steps_idx * (-2.0 * jnp.log(10000.0) / HS))
    angles = positions.astype(F32)[:, None] * inverse[None, :]
    cos = jnp.cos(angles)
    sin = jnp.where(lane % HS < HS // 2, -jnp.sin(angles), jnp.sin(angles))

    span = 128
    blocks = row_len // span
    first_begin = begins.reshape(blocks, span)[:, 0]
    ends = row_len + jnp.arange(blocks, dtype=jnp.int32) * span
    steps = jnp.maximum(ends - first_begin + 2 * span - 1, 0) // (2 * span)
    ids = jnp.arange(tok_count, dtype=jnp.int32)
    present = jnp.max((slabs.reshape(blocks, span)[:, :, None] == ids).astype(jnp.int32), axis=1)
    earlier = jnp.sum(jnp.where(ids[:, None] < ids[None, :], present[:, :, None], 0), axis=1)
    listed = (present[:, None, :] == 1) & (earlier[:, None, :] == ids[None, :, None])
    used = jnp.sum(jnp.where(listed, ids, 0), axis=2)
    used = jnp.concatenate([jnp.sum(present, axis=1, keepdims=True), used], axis=1)
    rows = jnp.concatenate([begins[None], slabs[None], jnp.zeros((6, row_len), jnp.int32)], axis=0)

    q, kv_now = project(gathered, w_query, w_keyval, cos, sin)
    kv_prev = lax.ppermute(kv_now, "tok", [(i, i + 1) for i in range(tok_count - 1)])
    partial = attend(q, kv_prev, kv_now, cache, rows, steps, used, slab_fill, w_out)
    hidden, arrived = settle(partial, tokens, ffn_gain[None], 2)
    answered = run_experts(arrived.reshape(-1, arrived.shape[-1]), gates_all, w_gate, w_up, w_down)
    return scatter_tok(answered.reshape(arrived.shape), hidden, 3)


def solution(mesh):
    return jax.shard_map(
        local,
        mesh=mesh,
        in_specs=(
            P(("tok", "head"), None),
            P(),
            P(),
            P(),
            P(),
            P("tok", "head"),
            P(),
            P(None, "head"),
            P(None, "head"),
            P("head", None),
            P(),
            P(("tok", "head"), None),
            P(("tok", "head"), None),
            P("tok", None, None),
            P("tok", None, None),
            P("tok", None, None),
        ),
        out_specs=P(("tok", "head"), None),
        check_vma=False,
    )
```

```python
import functools

import jax
import jax.numpy as jnp
from jax import lax
from jax.experimental import pallas as pl
from jax.experimental.pallas import tpu as pltpu
from jax.sharding import PartitionSpec as P

HS = 64
EXPERTS = 32
TOPK = 8
PREFIX = 512
NEG_FILL = -1e30
NORM_EPS = 1e-06
LOG2E = 1.4426950408889634
BF = jnp.bfloat16
F32 = jnp.float32
VMEM_CAP = 60 * 1024 * 1024


def rms_scale(values, gain):
    widened = values.astype(F32)
    spread = jnp.mean(widened * widened, axis=-1, keepdims=True)
    return widened * lax.rsqrt(spread + NORM_EPS) * gain


def request_tables(window, own, group_ids, prefix_owner, slab_fill):
    reqs = group_ids.shape[0]
    ids = jnp.arange(reqs, dtype=jnp.int32)
    slabs = jnp.arange(prefix_owner.shape[0], dtype=jnp.int32)
    begins = jnp.sum((window[None, :] < ids[:, None]).astype(jnp.int32), axis=1)
    slab_of = jnp.sum(jnp.where(group_ids[:, None] == slabs, prefix_owner, 0), axis=1)
    fill_of = jnp.sum(jnp.where(slab_of[:, None] == slabs, slab_fill, 0), axis=1)
    packed = (begins * 16 + slab_of) * 1024 + fill_of
    mine = jnp.sum(jnp.where(own[None, :] == ids[:, None], packed[:, None], 0), axis=0)
    return mine // (16 * 1024), (mine // 1024) % 16, mine % 1024


def turn(x, wq, wkv, cos, sin):
    both = jnp.concatenate(
        [
            lax.dot_general(x, wq, (((1,), (1,)), ((), ())), preferred_element_type=F32),
            jnp.dot(x, wkv, preferred_element_type=F32),
        ],
        axis=1,
    )
    width = both.shape[1]
    lane = lax.broadcasted_iota(jnp.int32, both.shape, 1)
    swapped = jnp.where(
        lane % HS < HS // 2,
        -pltpu.roll(both, width - HS // 2, 1),
        pltpu.roll(both, HS // 2, 1),
    )
    copies = -(-width // 128)
    cos = jnp.concatenate([cos] * copies, axis=1)[:, :width]
    sin = jnp.concatenate([sin] * copies, axis=1)[:, :width]
    return jnp.where(lane < wq.shape[0] + HS, both * cos + swapped * sin, both).astype(BF)


def attend_kernel(
    steps_ref, used_ref, fill_ref, q_ref, near_ref, cache_ref, rows_ref, wout_ref, out_ref
):
    block = pl.program_id(0)
    heads, span = q_ref.shape[0], q_ref.shape[1]
    row_len = near_ref.shape[0] // 2
    scale = HS ** (-0.5) * LOG2E

    queries = jnp.concatenate([q_ref[h] for h in range(heads)], axis=0)
    begins = jnp.concatenate([rows_ref[0:1]] * heads, axis=1)
    slabs = jnp.concatenate([rows_ref[1:2]] * heads, axis=1)
    offset = row_len + block * span
    wide = heads * span

    def scores(kv):
        return lax.dot_general(kv, queries, (((1,), (1,)), ((), ())), preferred_element_type=F32)

    def absorb(s, kv, carry):
        peak, total, acc = carry
        peak_new = jnp.maximum(peak, jnp.max(s, axis=0, keepdims=True))
        factor = jnp.exp2((peak - peak_new) * scale)
        weights = jnp.exp2((s - peak_new) * scale)
        total = total * factor + jnp.sum(weights, axis=0, keepdims=True)
        values = kv.T[HS:]
        acc = acc * factor + jnp.dot(values, weights.astype(BF), preferred_element_type=F32)
        return peak_new, total, acc

    kv = near_ref[pl.ds(pl.multiple_of(offset, span), span)]
    key = lax.broadcasted_iota(jnp.int32, (span, wide), 0)
    query = lax.broadcasted_iota(jnp.int32, (span, wide), 1) % span
    s = jnp.where((key <= query) & (key >= begins - offset), scores(kv), NEG_FILL)
    carry = (
        jnp.full((1, wide), NEG_FILL, F32),
        jnp.zeros((1, wide), F32),
        jnp.zeros((HS, wide), F32),
    )
    carry = absorb(s, kv, carry)

    chunk = 2 * span

    def near_step(step, carry):
        first = pl.multiple_of(offset - (step + 1) * chunk, span)
        kv = near_ref[pl.ds(first, chunk)]
        key = lax.broadcasted_iota(jnp.int32, (chunk, wide), 0)
        s = jnp.where(key >= begins - first, scores(kv), NEG_FILL)
        return absorb(s, kv, carry)

    carry = lax.fori_loop(0, steps_ref[block], near_step, carry)

    def far_step(step, carry):
        slab = used_ref[block, step + 1]
        kv = cache_ref[pl.ds(pl.multiple_of(slab * PREFIX, PREFIX), PREFIX)]
        key = lax.broadcasted_iota(jnp.int32, (PREFIX, wide), 0)
        limit = jnp.where(slabs == slab, fill_ref[slab], 0)
        s = jnp.where(key < limit, scores(kv), NEG_FILL)
        return absorb(s, kv, carry)

    _, total, acc = lax.fori_loop(0, used_ref[block, 0], far_step, carry)
    mixed = (acc / total).T
    mixed = jnp.concatenate([mixed[h * span : (h + 1) * span] for h in range(heads)], axis=1)
    out_ref[...] = jnp.dot(mixed.astype(BF), wout_ref[...], preferred_element_type=F32).astype(BF)


def attend(q, near, cache, rows, steps, used, fill, w_out, span=128):
    heads, length, _ = q.shape
    whole = lambda a: pl.BlockSpec(a.shape, lambda i, *_: (0,) * a.ndim)
    return pl.pallas_call(
        attend_kernel,
        grid_spec=pltpu.PrefetchScalarGridSpec(
            num_scalar_prefetch=3,
            grid=(length // span,),
            in_specs=[
                pl.BlockSpec((heads, span, 128), lambda i, *_: (0, i, 0)),
                whole(near),
                whole(cache),
                pl.BlockSpec((8, span), lambda i, *_: (0, i)),
                whole(w_out),
            ],
            out_specs=pl.BlockSpec((span, w_out.shape[1]), lambda i, *_: (i, 0)),
        ),
        out_shape=jax.ShapeDtypeStruct((length, w_out.shape[1]), BF),
        compiler_params=pltpu.CompilerParams(vmem_limit_bytes=VMEM_CAP),
        name="attend",
    )(steps, used, fill, q, near, cache, rows, w_out)


MESH_ID = pl.DeviceIdType.MESH


def torus_messages():
    keys = []
    for half in (0, 1):
        for sign in (1, -1):
            keys.append(("near", half, 0, sign))
            keys.append(("far", half, 0, sign))
            for a in (0, -1, 1, 2):
                keys.append(("side", half, a, sign))
                keys.append(("last", half, a, sign))
    return {key: i for i, key in enumerate(keys)}


def place_of(place, dx, dy):
    return ((place // 4 + dx + 4) % 4) * 4 + (place % 4 + dy + 4) % 4


def torus_gather(own, out, rows, sends, receives, keys):
    place, head = lax.axis_index("tok"), lax.axis_index("head")
    half_rows, part = rows // 2, rows // 4
    started = []

    def unit(half, a, b):
        return (a, b) if half == 0 else (b, a)

    def copy(key, landing=False):
        kind, half, a, sign = key
        first = kind in ("near", "far")
        if kind == "near":
            source = (0, 0)
        elif kind == "far":
            source = (-sign, 0)
        elif kind == "side":
            source = (a, 0)
        else:
            source = (a, -sign)
        begin, size = half * half_rows, half_rows
        if kind in ("far", "last"):
            begin, size = begin + (0 if sign == 1 else part), part
        if landing:
            source = (source[0] - sign, source[1]) if first else (source[0], source[1] - sign)
        slot = place_of(place, *unit(half, *source))
        step = unit(half, sign, 0) if first else unit(half, 0, sign)
        target = out.at[slot, pl.ds(begin, size)]
        if not landing and source == (0, 0):
            src = own.at[pl.ds(begin, size)]
        else:
            src = target
        return pltpu.make_async_remote_copy(
            src_ref=src,
            dst_ref=target,
            send_sem=sends.at[keys[key]],
            recv_sem=receives.at[keys[key]],
            device_id=(place_of(place, *step), head),
            device_id_type=MESH_ID,
        )

    def send(*key):
        c = copy(key)
        c.start()
        started.append(c)

    def arrive(*key):
        copy(key, landing=True).wait_recv()

    for sign in (1, -1):
        for half in (0, 1):
            send("near", half, 0, sign)
    for sign in (1, -1):
        for half in (0, 1):
            send("side", half, 0, sign)
    yield
    for sign in (1, -1):
        for half in (0, 1):
            arrive("near", half, 0, sign)
            send("far", half, 0, sign)
            send("side", half, -sign, 1)
            send("side", half, -sign, -1)
    yield
    for sign in (1, -1):
        for half in (0, 1):
            arrive("side", half, 0, sign)
            send("last", half, 0, sign)
    yield
    for half in (0, 1):
        for sign in (1, -1):
            arrive("far", half, 0, sign)
        for sign in (1, -1):
            send("side", half, 2, sign)
    yield
    for a in (-1, 1, 2):
        for sign in (1, -1):
            for half in (0, 1):
                arrive("side", half, a, sign)
                send("last", half, a, sign)
        yield
    for a in (0, -1, 1, 2):
        for half in (0, 1):
            for sign in (1, -1):
                arrive("last", half, a, sign)
    for c in started:
        c.wait_send()
    yield


def greet(peers):
    barrier = pltpu.get_barrier_semaphore()
    for peer in peers:
        pl.semaphore_signal(barrier, inc=1, device_id=peer, device_id_type=MESH_ID)
    pl.semaphore_wait(barrier, len(peers))


def torus_peers():
    place, head = lax.axis_index("tok"), lax.axis_index("head")
    return [(place_of(place, *s), head) for s in ((1, 0), (-1, 0), (0, 1), (0, -1))]


def scatter_messages():
    keys = []
    for half in (0, 1):
        for a in (2, -1, 1, 0):
            for sign in (1, -1):
                for kind in ("far", "plain", "added"):
                    keys.append((kind, half, a, sign))
        for sign in (1, -1):
            for kind in ("far2", "plain2", "added2"):
                keys.append((kind, half, 0, sign))
    return {key: i for i, key in enumerate(keys)}


class TorusScatter:
    def __init__(self, parts, land, rows, sends, receives):
        self.parts, self.land, self.sends, self.receives = parts, land, sends, receives
        self.keys = scatter_messages()
        self.rows = rows
        self.place, self.head = lax.axis_index("tok"), lax.axis_index("head")

    def slot(self, half, a, b):
        return place_of(self.place, *((a, b) if half == 0 else (b, a)))

    def spot(self, kind, half, a, sign):
        base, part = half * self.rows // 2, self.rows // 4
        low, high = pl.ds(base, part), pl.ds(base + part, part)
        with_far, plain = (low, high) if sign == 1 else (high, low)
        distance = 2 if kind.startswith("far") else sign
        offset = (distance, 0) if kind.endswith("2") else (a, distance)
        return self.slot(half, *offset), plain if kind.startswith("plain") else with_far

    def copy(self, *key):
        kind, half, a, sign = key
        slot, rows_of = self.spot(*key)
        step = (sign, 0) if kind.endswith("2") else (0, sign)
        return pltpu.make_async_remote_copy(
            src_ref=self.parts.at[slot, rows_of],
            dst_ref=self.land.at[self.keys[key]],
            send_sem=self.sends.at[self.keys[key]],
            recv_sem=self.receives.at[self.keys[key]],
            device_id=(self.slot(half, *step), self.head),
            device_id_type=MESH_ID,
        )

    def send(self, *key):
        self.copy(*key).start()

    def add(self, key, slot, rows_of):
        self.copy(*key).wait_recv()
        self.parts[slot, rows_of] = (
            self.parts[slot, rows_of].astype(F32) + self.land[self.keys[key]].astype(F32)
        ).astype(self.parts.dtype)

    def send_unit(self, dx, dy):
        for half, a, b in ((0, dx, dy), (1, dy, dx)):
            if b == 2:
                self.send("far", half, a, 1)
                self.send("far", half, a, -1)
            elif b != 0:
                self.send("plain", half, a, b)

    def pass_on(self, half, a):
        for sign in (1, -1):
            slot, rows_of = self.spot("added", half, a, sign)
            self.add(("far", half, a, sign), slot, rows_of)
            self.send("added", half, a, sign)

    def complete(self, half, a):
        slot = self.slot(half, a, 0)
        for sign in (1, -1):
            for kind in ("plain", "added"):
                _, rows_of = self.spot(kind, half, a, sign)
                self.add((kind, half, a, sign), slot, rows_of)
        if a == 2:
            self.send("far2", half, 0, 1)
            self.send("far2", half, 0, -1)
        elif a != 0:
            self.send("plain2", half, 0, a)

    def pass_on_last(self, half):
        for sign in (1, -1):
            slot, rows_of = self.spot("added2", half, 0, sign)
            self.add(("far2", half, 0, sign), slot, rows_of)
            self.send("added2", half, 0, sign)

    def finish(self):
        for kind in ("plain2", "added2"):
            for half in (0, 1):
                for sign in (1, -1):
                    _, rows_of = self.spot(kind, half, 0, sign)
                    self.add((kind, half, 0, sign), self.place, rows_of)

    def drain(self):
        for key in self.keys:
            self.copy(*key).wait_send()


PAIRS = (
    ((2, 2), (2, -1)),
    ((-1, 2), (2, 1)),
    ((1, 2), (2, 0)),
    ((0, 2), (-1, -1)),
    ((1, -1), (-1, 1)),
    ((1, 1), (-1, 0)),
    ((0, -1), (1, 0)),
    ((0, 1), (0, 0)),
)


def pair_slot(place, step, member):
    dx, dy = 0, 0
    for k, pair in enumerate(PAIRS):
        dx = jnp.where(step == k, pair[member][0], dx)
        dy = jnp.where(step == k, pair[member][1], dy)
    return place_of(place, dx, dy)


def experts_kernel(
    x_ref, gates_ref, wg_ref, wu_ref, wd_ref, hidden_ref, out_ref, parts, land, held, sends, receives, load_sems
):
    place = lax.axis_index("tok")
    rows = parts.shape[1]

    def load(step, side, member):
        return pltpu.make_async_copy(
            x_ref.at[pair_slot(place, step, member)],
            held.at[side, pl.ds(member * rows, rows)],
            load_sems.at[side, member],
        )

    for member in (0, 1):
        load(0, 0, member).start()
    greet(torus_peers())
    back = TorusScatter(parts, land, rows, sends, receives)

    @pl.loop(0, len(PAIRS))
    def _(step):
        side = step % 2
        for member in (0, 1):
            load(step, side, member).wait()

        @pl.when(step < len(PAIRS) - 1)
        def _():
            for member in (0, 1):
                load(step + 1, 1 - side, member).start()

        slots = [pair_slot(place, step, member) for member in (0, 1)]
        gates = jnp.concatenate([gates_ref[s].T for s in slots], axis=0)
        x = held[side]
        total = jnp.zeros((2 * rows, wd_ref.shape[2]), F32)
        for e in range(wg_ref.shape[0]):
            g = jnp.dot(x, wg_ref[e], preferred_element_type=F32)
            u = jnp.dot(x, wu_ref[e], preferred_element_type=F32)
            act = (g / (1.0 + jnp.exp(-g)) * u).astype(BF)
            o = jnp.dot(act, wd_ref[e], preferred_element_type=F32).astype(BF).astype(F32)
            total = total + gates[:, e : e + 1] * o
        for member in (0, 1):
            parts[slots[member]] = total[member * rows : (member + 1) * rows].astype(BF)
        for k, pair in enumerate(PAIRS):

            @pl.when(step == k)
            def _():
                for unit in pair:
                    back.send_unit(*unit)
                if k == 3:
                    for half in (0, 1):
                        back.pass_on(half, 2)
                if k == 5:
                    for half in (0, 1):
                        for a in (-1, 1):
                            back.pass_on(half, a)
                    for half in (0, 1):
                        back.complete(half, 2)

    for half in (0, 1):
        back.pass_on(half, 0)
    for half in (0, 1):
        for a in (-1, 1):
            back.complete(half, a)
    for half in (0, 1):
        back.pass_on_last(half)
    for half in (0, 1):
        back.complete(half, 0)
    back.finish()
    back.drain()
    out_ref[...] = (hidden_ref[...] + parts[place].astype(F32)).astype(out_ref.dtype)


def run_experts(x, gates, w_gate, w_up, w_down, hidden, collective_id):
    count = len(scatter_messages())
    _, rows, width = x.shape
    dma = pltpu.SemaphoreType.DMA
    vmem = pl.BlockSpec(memory_space=pltpu.VMEM)
    return pl.pallas_call(
        experts_kernel,
        in_specs=[pl.BlockSpec(memory_space=pl.ANY)] + [vmem] * 5,
        out_specs=vmem,
        out_shape=jax.ShapeDtypeStruct((rows, width), x.dtype),
        scratch_shapes=[
            pltpu.VMEM(x.shape, x.dtype),
            pltpu.VMEM((count, rows // 4, width), x.dtype),
            pltpu.VMEM((2, 2 * rows, width), x.dtype),
            dma((count,)),
            dma((count,)),
            dma((2, 2)),
        ],
        compiler_params=pltpu.CompilerParams(
            collective_id=collective_id, has_side_effects=True, vmem_limit_bytes=VMEM_CAP
        ),
        name="experts",
    )(x, gates, w_gate, w_up, w_down, hidden)


def ring_messages(kinds):
    return {key: i for i, key in enumerate(kinds)}


GATHER_RING = ring_messages(
    [("near", 1), ("near", -1), ("far", 1), ("far", -1), ("pair", 0), ("pair", 1), ("pair", -1), ("half", 1), ("half", -1)]
)
SCATTER_RING = ring_messages(
    [("pair", 2), ("pair", 1), ("pair", -1), ("pair", 0)]
    + [(kind, sign) for kind in ("far", "plain", "added") for sign in (1, -1)]
)


def head_of(head, dz, flip=0):
    core = head % 2
    return ((head // 2 + dz + 4) % 4) * 2 + (core + flip) % 2


def ring_peers():
    place, head = lax.axis_index("tok"), lax.axis_index("head")
    return [(place, head_of(head, 1)), (place, head_of(head, -1)), (place, head_of(head, 0, 1))]


def ring_gather(own, out, rows, sends, receives, keys):
    place, head = lax.axis_index("tok"), lax.axis_index("head")
    started = []

    def copy(key, landing=False):
        kind, value = key
        begin, size = 0, rows
        if kind in ("far", "half"):
            size = rows // 2
            begin = 0 if value == 1 else size
        dz = {"near": 0, "far": -value, "pair": value, "half": 2}[kind]
        crossing = kind in ("pair", "half")
        if landing:
            slot = head_of(head, dz, 1) if crossing else head_of(head, dz - value)
        else:
            slot = head_of(head, dz)
        target = out.at[slot, pl.ds(begin, size)]
        src = own.at[pl.ds(begin, size)] if not landing and dz == 0 else target
        peer = head_of(head, 0, 1) if crossing else head_of(head, value)
        return pltpu.make_async_remote_copy(
            src_ref=src,
            dst_ref=target,
            send_sem=sends.at[keys[key]],
            recv_sem=receives.at[keys[key]],
            device_id=(place, peer),
            device_id_type=MESH_ID,
        )

    def send(*key):
        c = copy(key)
        c.start()
        started.append(c)

    def arrive(*key):
        copy(key, landing=True).wait_recv()

    send("near", 1)
    send("near", -1)
    send("pair", 0)
    yield
    arrive("pair", 0)
    yield
    for sign in (1, -1):
        arrive("near", sign)
        send("far", sign)
        send("pair", -sign)
    yield
    for dz in (1, -1):
        arrive("pair", dz)
    yield
    for sign in (1, -1):
        arrive("far", sign)
        send("half", sign)
    yield
    for sign in (1, -1):
        arrive("half", sign)
    for c in started:
        c.wait_send()
    yield


def opening_kernel(
    x_ref, cache_ref, gates_ref, wq_ref, wkv_ref, angles_ref, q_ref, near_ref, cache_out, gates_out,
    gathered, cos_ref, sin_ref, ts, tr, hs, hr, gs, gr, ks, kr, own_sems,
):
    place, head = lax.axis_index("tok"), lax.axis_index("head")
    count = gates_ref.shape[0]
    rows = x_ref.shape[0]
    row_len = near_ref.shape[0] // 2
    heads = q_ref.shape[0]
    others = [((place + d) % count, head) for d in range(1, count)]
    greet(others + ring_peers())
    mine = [
        pltpu.make_async_copy(cache_ref, cache_out.at[place], own_sems.at[0]),
        pltpu.make_async_copy(gates_ref.at[place], gates_out.at[place], own_sems.at[1]),
    ]
    one = ring_gather(x_ref, gathered, rows, hs, hr, GATHER_RING)
    two = torus_gather(cache_ref, cache_out, cache_ref.shape[0], ts, tr, torus_messages())

    def gate_copy(d, landing=False):
        target = (place + d) % count
        slot = (place - d + count) % count if landing else place
        return pltpu.make_async_remote_copy(
            src_ref=gates_ref.at[target],
            dst_ref=gates_out.at[slot],
            send_sem=gs.at[d],
            recv_sem=gr.at[d],
            device_id=(target, head),
            device_id_type=MESH_ID,
        )

    def onward(block):
        at = pl.multiple_of(block * rows, rows)
        return pltpu.make_async_remote_copy(
            src_ref=near_ref.at[pl.ds(row_len + at, rows)],
            dst_ref=near_ref.at[pl.ds(at, rows)],
            send_sem=ks.at[block],
            recv_sem=kr.at[block],
            device_id=((place + 1) % count, head),
            device_id_type=MESH_ID,
        )

    def project(block, x):
        at = pl.multiple_of(block * rows, rows)
        here = pl.ds(at, rows)
        turned = turn(x, wq_ref[...], wkv_ref[...], cos_ref[here], sin_ref[here])
        pad = jnp.zeros((rows, HS), BF)
        for h in range(heads):
            q_ref[h, here] = jnp.concatenate([turned[:, h * HS : (h + 1) * HS], pad], axis=1)
        near_ref[pl.ds(row_len + at, rows)] = turned[:, heads * HS :]
        onward(block).start()

    next(one)
    next(two)
    for c in mine:
        c.start()
    for d in range(1, count):
        gate_copy(d).start()
    half = HS // 2
    cos, sin = angles_ref[:half].T, angles_ref[half:].T
    cos_ref[...] = jnp.concatenate([cos] * 4, axis=1)
    sin_ref[...] = jnp.concatenate([sin] * 4, axis=1)

    def project_slots(*slots):
        for block in slots:
            project(block, gathered[block])

    project(head, x_ref[...])
    next(two)
    next(one)
    project_slots(head_of(head, 0, 1))
    next(two)
    next(two)
    next(one)
    project_slots(head_of(head, 1), head_of(head, -1))
    next(one)
    project_slots(head_of(head, 1, 1), head_of(head, -1, 1))
    next(two)
    next(two)
    next(one)
    project_slots(head_of(head, 2))
    next(two)
    next(one)
    project_slots(head_of(head, 2, 1))
    for _ in two:
        pass
    for d in range(1, count):
        gate_copy(d, True).wait_recv()
    for d in range(1, count):
        gate_copy(d).wait_send()
    for c in mine:
        c.wait()
    for dz in range(4):
        for flip in (0, 1):
            onward(head_of(head, dz, flip)).wait_recv()
    for dz in range(4):
        for flip in (0, 1):
            onward(head_of(head, dz, flip)).wait_send()


def opening(x, cache, gates, w_query, w_keyval, angles, collective_id):
    t, r, n = len(torus_messages()), len(GATHER_RING), gates.shape[0]
    rows, width = x.shape
    length = angles.shape[1]
    heads = w_query.shape[0] // HS
    dma = pltpu.SemaphoreType.DMA
    vmem, anywhere = pl.BlockSpec(memory_space=pltpu.VMEM), pl.BlockSpec(memory_space=pl.ANY)
    return pl.pallas_call(
        opening_kernel,
        in_specs=[vmem] * 6,
        out_specs=[vmem, vmem, anywhere, anywhere],
        out_shape=[
            jax.ShapeDtypeStruct((heads, length, 128), BF),
            jax.ShapeDtypeStruct((2 * length, 128), BF),
            jax.ShapeDtypeStruct((n,) + cache.shape, cache.dtype),
            jax.ShapeDtypeStruct(gates.shape, gates.dtype),
        ],
        scratch_shapes=[
            pltpu.VMEM((length // rows, rows, width), BF),
            pltpu.VMEM((length, 128), F32),
            pltpu.VMEM((length, 128), F32),
            dma((t,)),
            dma((t,)),
            dma((r,)),
            dma((r,)),
            dma((n,)),
            dma((n,)),
            dma((length // rows,)),
            dma((length // rows,)),
            dma((2,)),
        ],
        compiler_params=pltpu.CompilerParams(
            collective_id=collective_id, has_side_effects=True, vmem_limit_bytes=VMEM_CAP
        ),
        name="opening",
    )(x, cache, gates, w_query, w_keyval, angles)


def ring_scatter(parts, pair_land, land, rows, sends, receives, keys):
    place, head = lax.axis_index("tok"), lax.axis_index("head")
    started = []
    low, high = pl.ds(0, rows // 2), pl.ds(rows // 2, rows // 2)

    def spot(key):
        kind, value = key
        if kind == "far":
            return head_of(head, 2), (low if value == 1 else high)
        if kind == "plain":
            return head_of(head, value), (high if value == 1 else low)
        return head_of(head, value), (low if value == 1 else high)

    def copy(key):
        kind, value = key
        if kind == "pair":
            src, dst = parts.at[head_of(head, value, 1)], pair_land.at[keys[key]]
            peer = head_of(head, 0, 1)
        else:
            slot, rows_of = spot(key)
            src, dst = parts.at[slot, rows_of], land.at[keys[key] - 4]
            peer = head_of(head, value)
        return pltpu.make_async_remote_copy(
            src_ref=src,
            dst_ref=dst,
            send_sem=sends.at[keys[key]],
            recv_sem=receives.at[keys[key]],
            device_id=(place, peer),
            device_id_type=MESH_ID,
        )

    def send(*key):
        c = copy(key)
        c.start()
        started.append(c)

    def add(key, slot, rows_of, buffer, index):
        copy(key).wait_recv()
        parts[slot, rows_of] = (parts[slot, rows_of].astype(F32) + buffer[index].astype(F32)).astype(parts.dtype)

    def add_pair(dz):
        key = ("pair", dz)
        add(key, head_of(head, dz), pl.ds(0, rows), pair_land, keys[key])

    for dz in (2, 1, -1, 0):
        send("pair", dz)
    add_pair(2)
    for sign in (1, -1):
        send("far", sign)
    for sign in (1, -1):
        add_pair(sign)
        send("plain", sign)
    add_pair(0)
    for sign in (1, -1):
        key = ("far", sign)
        slot, rows_of = spot(("added", sign))
        add(key, slot, rows_of, land, keys[key] - 4)
        send("added", sign)
    for kind in ("plain", "added"):
        for sign in (1, -1):
            key = (kind, sign)
            _, rows_of = spot(key)
            add(key, head, rows_of, land, keys[key] - 4)
    for c in started:
        c.wait_send()


def settle_kernel(
    part_ref, tokens_ref, gain_ref, hidden_ref, out_ref, parts, pair_land, land, normed, rs, rr, ts, tr, own_sems
):
    place, head = lax.axis_index("tok"), lax.axis_index("head")
    rows = tokens_ref.shape[0]
    loads = [
        pltpu.make_async_copy(part_ref.at[pl.ds(h * rows, rows)], parts.at[h], own_sems.at[h]) for h in range(8)
    ]
    for c in loads:
        c.start()
    greet(torus_peers() + ring_peers())
    for c in loads:
        c.wait()
    ring_scatter(parts, pair_land, land, rows, rs, rr, SCATTER_RING)
    hidden = tokens_ref[...].astype(F32) + parts[head].astype(F32)
    hidden_ref[...] = hidden
    normed[...] = rms_scale(hidden, gain_ref[...]).astype(normed.dtype)
    mine = pltpu.make_async_copy(normed, out_ref.at[place], own_sems.at[8])
    mine.start()
    for _ in torus_gather(normed, out_ref, rows, ts, tr, torus_messages()):
        pass
    mine.wait()


def settle(partial, tokens, gain, collective_id):
    rows, width = tokens.shape
    t, r = len(torus_messages()), len(SCATTER_RING)
    dma = pltpu.SemaphoreType.DMA
    return pl.pallas_call(
        settle_kernel,
        in_specs=[
            pl.BlockSpec(memory_space=pl.ANY),
            pl.BlockSpec(memory_space=pltpu.VMEM),
            pl.BlockSpec(memory_space=pltpu.VMEM),
        ],
        out_specs=[pl.BlockSpec(memory_space=pltpu.VMEM), pl.BlockSpec(memory_space=pl.ANY)],
        out_shape=[
            jax.ShapeDtypeStruct((rows, width), F32),
            jax.ShapeDtypeStruct((16, rows, width), BF),
        ],
        scratch_shapes=[
            pltpu.VMEM((8, rows, width), BF),
            pltpu.VMEM((4, rows, width), BF),
            pltpu.VMEM((6, rows // 2, width), BF),
            pltpu.VMEM((rows, width), BF),
            dma((r,)),
            dma((r,)),
            dma((t,)),
            dma((t,)),
            dma((9,)),
        ],
        compiler_params=pltpu.CompilerParams(
            collective_id=collective_id, has_side_effects=True, vmem_limit_bytes=VMEM_CAP
        ),
        name="settle",
    )(partial, tokens, gain)


def local(
    tokens,
    segments,
    group_ids,
    prefix_owner,
    slab_fill,
    prefix_cache,
    attn_gain,
    w_query,
    w_keyval,
    w_out,
    ffn_gain,
    routes,
    route_gates,
    w_gate,
    w_up,
    w_down,
):
    tok_count = lax.axis_size("tok")
    head_count = lax.axis_size("head")
    place = lax.axis_index("tok")
    row_len = tokens.shape[0] * head_count
    normed = rms_scale(tokens, attn_gain).astype(BF)
    exp_local = w_gate.shape[0]
    experts = jnp.arange(EXPERTS, dtype=jnp.int32)[:, None, None]
    gates = jnp.sum(jnp.where(routes.T[None] == experts, route_gates.T[None], 0.0), axis=1)
    gates = gates.reshape(tok_count, exp_local, -1)
    gates = jnp.concatenate([gates, jnp.zeros((tok_count, 8 - exp_local, gates.shape[2]), F32)], axis=1)

    padded = jnp.concatenate([jnp.full((row_len,), -1, jnp.int32), segments])
    window = lax.dynamic_slice_in_dim(padded, place * row_len, 2 * row_len, 0)
    own = window[row_len:]
    begins, slabs, fills = request_tables(window, own, group_ids, prefix_owner, slab_fill)
    positions = fills + row_len + jnp.arange(row_len, dtype=jnp.int32) - begins
    steps_idx = jnp.arange(HS // 2, dtype=F32)
    inverse = jnp.exp(steps_idx * (-2.0 * jnp.log(10000.0) / HS))
    angles = inverse[:, None] * positions.astype(F32)[None, :]
    turns = jnp.concatenate([jnp.cos(angles), jnp.sin(angles)], axis=0)
    q, near, cache, gates_all = opening(normed, prefix_cache, gates, w_query.T, w_keyval, turns, 1)
    cache = cache.reshape(-1, cache.shape[-1])

    span = 128
    blocks = row_len // span
    first_begin = begins.reshape(blocks, span)[:, 0]
    ends = row_len + jnp.arange(blocks, dtype=jnp.int32) * span
    steps = jnp.maximum(ends - first_begin + 2 * span - 1, 0) // (2 * span)
    ids = jnp.arange(tok_count, dtype=jnp.int32)
    present = jnp.max((slabs.reshape(blocks, span)[:, :, None] == ids).astype(jnp.int32), axis=1)
    earlier = jnp.sum(jnp.where(ids[:, None] < ids[None, :], present[:, :, None], 0), axis=1)
    listed = (present[:, None, :] == 1) & (earlier[:, None, :] == ids[None, :, None])
    used = jnp.sum(jnp.where(listed, ids, 0), axis=2)
    used = jnp.concatenate([jnp.sum(present, axis=1, keepdims=True), used], axis=1)
    rows = jnp.concatenate([begins[None], slabs[None], jnp.zeros((6, row_len), jnp.int32)], axis=0)

    partial = attend(q, near, cache, rows, steps, used, slab_fill, w_out)
    hidden, arrived = settle(partial, tokens, ffn_gain[None], 2)
    return run_experts(arrived, gates_all, w_gate, w_up, w_down, hidden, 3)


def solution(mesh):
    return jax.shard_map(
        local,
        mesh=mesh,
        in_specs=(
            P(("tok", "head"), None),
            P(),
            P(),
            P(),
            P(),
            P("tok", "head"),
            P(),
            P(None, "head"),
            P(None, "head"),
            P("head", None),
            P(),
            P(("tok", "head"), None),
            P(("tok", "head"), None),
            P("tok", None, None),
            P("tok", None, None),
            P("tok", None, None),
        ),
        out_specs=P(("tok", "head"), None),
        check_vma=False,
    )
```

```python
import functools

import jax
import jax.numpy as jnp
from jax import lax
from jax.experimental import pallas as pl
from jax.experimental.pallas import tpu as pltpu
from jax.sharding import PartitionSpec as P

HS = 64
EXPERTS = 32
TOPK = 8
PREFIX = 512
NEG_FILL = -1e30
NORM_EPS = 1e-06
LOG2E = 1.4426950408889634
BF = jnp.bfloat16
F32 = jnp.float32
VMEM_CAP = 60 * 1024 * 1024


def rms_scale(values, gain):
    widened = values.astype(F32)
    spread = jnp.mean(widened * widened, axis=-1, keepdims=True)
    return widened * lax.rsqrt(spread + NORM_EPS) * gain


def request_tables(window, own, group_ids, prefix_owner, slab_fill):
    reqs = group_ids.shape[0]
    ids = jnp.arange(reqs, dtype=jnp.int32)
    slabs = jnp.arange(prefix_owner.shape[0], dtype=jnp.int32)
    begins = jnp.sum((window[None, :] < ids[:, None]).astype(jnp.int32), axis=1)
    slab_of = jnp.sum(jnp.where(group_ids[:, None] == slabs, prefix_owner, 0), axis=1)
    fill_of = jnp.sum(jnp.where(slab_of[:, None] == slabs, slab_fill, 0), axis=1)
    packed = (begins * 16 + slab_of) * 1024 + fill_of
    mine = jnp.sum(jnp.where(own[None, :] == ids[:, None], packed[:, None], 0), axis=0)
    return mine // (16 * 1024), (mine // 1024) % 16, mine % 1024


def turn(x, wq, wkv, cos, sin):
    both = jnp.concatenate(
        [
            lax.dot_general(x, wq, (((1,), (1,)), ((), ())), preferred_element_type=F32),
            jnp.dot(x, wkv, preferred_element_type=F32),
        ],
        axis=1,
    )
    width = both.shape[1]
    lane = lax.broadcasted_iota(jnp.int32, both.shape, 1)
    swapped = jnp.where(
        lane % HS < HS // 2,
        -pltpu.roll(both, width - HS // 2, 1),
        pltpu.roll(both, HS // 2, 1),
    )
    copies = -(-width // 128)
    cos = jnp.concatenate([cos] * copies, axis=1)[:, :width]
    sin = jnp.concatenate([sin] * copies, axis=1)[:, :width]
    return jnp.where(lane < wq.shape[0] + HS, both * cos + swapped * sin, both).astype(BF)


def attend_kernel(
    steps_ref, used_ref, fill_ref, q_ref, near_ref, cache_ref, rows_ref, wout_ref, out_ref
):
    block = pl.program_id(0)
    heads, span = q_ref.shape[0], q_ref.shape[1]
    row_len = near_ref.shape[0] // 2
    scale = HS ** (-0.5) * LOG2E

    queries = jnp.concatenate([q_ref[h] for h in range(heads)], axis=0)
    begins = jnp.concatenate([rows_ref[0:1]] * heads, axis=1)
    slabs = jnp.concatenate([rows_ref[1:2]] * heads, axis=1)
    offset = row_len + block * span
    wide = heads * span

    def scores(kv):
        return lax.dot_general(kv, queries, (((1,), (1,)), ((), ())), preferred_element_type=F32)

    def absorb(s, kv, carry):
        peak, total, acc = carry
        peak_new = jnp.maximum(peak, jnp.max(s, axis=0, keepdims=True))
        factor = jnp.exp2((peak - peak_new) * scale)
        weights = jnp.exp2((s - peak_new) * scale)
        total = total * factor + jnp.sum(weights, axis=0, keepdims=True)
        values = kv.T[HS:]
        acc = acc * factor + jnp.dot(values, weights.astype(BF), preferred_element_type=F32)
        return peak_new, total, acc

    kv = near_ref[pl.ds(pl.multiple_of(offset, span), span)]
    key = lax.broadcasted_iota(jnp.int32, (span, wide), 0)
    query = lax.broadcasted_iota(jnp.int32, (span, wide), 1) % span
    s = jnp.where((key <= query) & (key >= begins - offset), scores(kv), NEG_FILL)
    carry = (
        jnp.full((1, wide), NEG_FILL, F32),
        jnp.zeros((1, wide), F32),
        jnp.zeros((HS, wide), F32),
    )
    carry = absorb(s, kv, carry)

    chunk = 2 * span

    def near_step(step, carry):
        first = pl.multiple_of(offset - (step + 1) * chunk, span)
        kv = near_ref[pl.ds(first, chunk)]
        key = lax.broadcasted_iota(jnp.int32, (chunk, wide), 0)
        s = jnp.where(key >= begins - first, scores(kv), NEG_FILL)
        return absorb(s, kv, carry)

    carry = lax.fori_loop(0, steps_ref[block], near_step, carry)

    def far_step(step, carry):
        slab = used_ref[block, step + 1]
        kv = cache_ref[pl.ds(pl.multiple_of(slab * PREFIX, PREFIX), PREFIX)]
        key = lax.broadcasted_iota(jnp.int32, (PREFIX, wide), 0)
        limit = jnp.where(slabs == slab, fill_ref[slab], 0)
        s = jnp.where(key < limit, scores(kv), NEG_FILL)
        return absorb(s, kv, carry)

    _, total, acc = lax.fori_loop(0, used_ref[block, 0], far_step, carry)
    mixed = (acc / total).T
    mixed = jnp.concatenate([mixed[h * span : (h + 1) * span] for h in range(heads)], axis=1)
    out_ref[...] = jnp.dot(mixed.astype(BF), wout_ref[...], preferred_element_type=F32).astype(BF)


def attend(q, near, cache, rows, steps, used, fill, w_out, span=128):
    heads, length, _ = q.shape
    whole = lambda a: pl.BlockSpec(a.shape, lambda i, *_: (0,) * a.ndim)
    return pl.pallas_call(
        attend_kernel,
        grid_spec=pltpu.PrefetchScalarGridSpec(
            num_scalar_prefetch=3,
            grid=(length // span,),
            in_specs=[
                pl.BlockSpec((heads, span, 128), lambda i, *_: (0, i, 0)),
                whole(near),
                whole(cache),
                pl.BlockSpec((8, span), lambda i, *_: (0, i)),
                whole(w_out),
            ],
            out_specs=pl.BlockSpec((span, w_out.shape[1]), lambda i, *_: (i, 0)),
        ),
        out_shape=jax.ShapeDtypeStruct((length, w_out.shape[1]), BF),
        compiler_params=pltpu.CompilerParams(vmem_limit_bytes=VMEM_CAP),
        name="attend",
    )(steps, used, fill, q, near, cache, rows, w_out)


MESH_ID = pl.DeviceIdType.MESH


def torus_messages():
    keys = []
    for half in (0, 1):
        for sign in (1, -1):
            keys.append(("near", half, 0, sign))
            keys.append(("far", half, 0, sign))
            for a in (0, -1, 1, 2):
                keys.append(("side", half, a, sign))
                keys.append(("last", half, a, sign))
    return {key: i for i, key in enumerate(keys)}


def place_of(place, dx, dy):
    return ((place // 4 + dx + 4) % 4) * 4 + (place % 4 + dy + 4) % 4


def torus_gather(own, out, rows, sends, receives, keys):
    place, head = lax.axis_index("tok"), lax.axis_index("head")
    half_rows, part = rows // 2, rows // 4
    started = []

    def unit(half, a, b):
        return (a, b) if half == 0 else (b, a)

    def copy(key, landing=False):
        kind, half, a, sign = key
        first = kind in ("near", "far")
        if kind == "near":
            source = (0, 0)
        elif kind == "far":
            source = (-sign, 0)
        elif kind == "side":
            source = (a, 0)
        else:
            source = (a, -sign)
        begin, size = half * half_rows, half_rows
        if kind in ("far", "last"):
            begin, size = begin + (0 if sign == 1 else part), part
        if landing:
            source = (source[0] - sign, source[1]) if first else (source[0], source[1] - sign)
        slot = place_of(place, *unit(half, *source))
        step = unit(half, sign, 0) if first else unit(half, 0, sign)
        target = out.at[slot, pl.ds(begin, size)]
        if not landing and source == (0, 0):
            src = own.at[pl.ds(begin, size)]
        else:
            src = target
        return pltpu.make_async_remote_copy(
            src_ref=src,
            dst_ref=target,
            send_sem=sends.at[keys[key]],
            recv_sem=receives.at[keys[key]],
            device_id=(place_of(place, *step), head),
            device_id_type=MESH_ID,
        )

    def send(*key):
        c = copy(key)
        c.start()
        started.append(c)

    def arrive(*key):
        copy(key, landing=True).wait_recv()

    for sign in (1, -1):
        for half in (0, 1):
            send("near", half, 0, sign)
    for sign in (1, -1):
        for half in (0, 1):
            send("side", half, 0, sign)
    yield
    for sign in (1, -1):
        for half in (0, 1):
            arrive("near", half, 0, sign)
            send("far", half, 0, sign)
            send("side", half, -sign, 1)
            send("side", half, -sign, -1)
    yield
    for sign in (1, -1):
        for half in (0, 1):
            arrive("side", half, 0, sign)
            send("last", half, 0, sign)
    yield
    for half in (0, 1):
        for sign in (1, -1):
            arrive("far", half, 0, sign)
        for sign in (1, -1):
            send("side", half, 2, sign)
    yield
    for a in (-1, 1, 2):
        for sign in (1, -1):
            for half in (0, 1):
                arrive("side", half, a, sign)
                send("last", half, a, sign)
        yield
    for a in (0, -1, 1, 2):
        for half in (0, 1):
            for sign in (1, -1):
                arrive("last", half, a, sign)
    for c in started:
        c.wait_send()
    yield


def greet(peers):
    barrier = pltpu.get_barrier_semaphore()
    for peer in peers:
        pl.semaphore_signal(barrier, inc=1, device_id=peer, device_id_type=MESH_ID)
    pl.semaphore_wait(barrier, len(peers))


def torus_peers():
    place, head = lax.axis_index("tok"), lax.axis_index("head")
    return [(place_of(place, *s), head) for s in ((1, 0), (-1, 0), (0, 1), (0, -1))]


def scatter_messages():
    keys = []
    for half in (0, 1):
        for a in (2, -1, 1, 0):
            for sign in (1, -1):
                for kind in ("far", "plain", "added"):
                    keys.append((kind, half, a, sign))
        for sign in (1, -1):
            for kind in ("far2", "plain2", "added2"):
                keys.append((kind, half, 0, sign))
    return {key: i for i, key in enumerate(keys)}


class TorusScatter:
    def __init__(self, parts, land, rows, sends, receives):
        self.parts, self.land, self.sends, self.receives = parts, land, sends, receives
        self.keys = scatter_messages()
        self.rows = rows
        self.place, self.head = lax.axis_index("tok"), lax.axis_index("head")

    def slot(self, half, a, b):
        return place_of(self.place, *((a, b) if half == 0 else (b, a)))

    def spot(self, kind, half, a, sign):
        base, part = half * self.rows // 2, self.rows // 4
        low, high = pl.ds(base, part), pl.ds(base + part, part)
        with_far, plain = (low, high) if sign == 1 else (high, low)
        distance = 2 if kind.startswith("far") else sign
        offset = (distance, 0) if kind.endswith("2") else (a, distance)
        return self.slot(half, *offset), plain if kind.startswith("plain") else with_far

    def copy(self, *key):
        kind, half, a, sign = key
        slot, rows_of = self.spot(*key)
        step = (sign, 0) if kind.endswith("2") else (0, sign)
        return pltpu.make_async_remote_copy(
            src_ref=self.parts.at[slot, rows_of],
            dst_ref=self.land.at[self.keys[key]],
            send_sem=self.sends.at[self.keys[key]],
            recv_sem=self.receives.at[self.keys[key]],
            device_id=(self.slot(half, *step), self.head),
            device_id_type=MESH_ID,
        )

    def send(self, *key):
        self.copy(*key).start()

    def add(self, key, slot, rows_of):
        self.copy(*key).wait_recv()
        self.parts[slot, rows_of] = (
            self.parts[slot, rows_of].astype(F32) + self.land[self.keys[key]].astype(F32)
        ).astype(self.parts.dtype)

    def send_unit(self, dx, dy):
        for half, a, b in ((0, dx, dy), (1, dy, dx)):
            if b == 2:
                self.send("far", half, a, 1)
                self.send("far", half, a, -1)
            elif b != 0:
                self.send("plain", half, a, b)

    def pass_on(self, half, a):
        for sign in (1, -1):
            slot, rows_of = self.spot("added", half, a, sign)
            self.add(("far", half, a, sign), slot, rows_of)
            self.send("added", half, a, sign)

    def complete(self, half, a):
        slot = self.slot(half, a, 0)
        for sign in (1, -1):
            for kind in ("plain", "added"):
                _, rows_of = self.spot(kind, half, a, sign)
                self.add((kind, half, a, sign), slot, rows_of)
        if a == 2:
            self.send("far2", half, 0, 1)
            self.send("far2", half, 0, -1)
        elif a != 0:
            self.send("plain2", half, 0, a)

    def pass_on_last(self, half):
        for sign in (1, -1):
            slot, rows_of = self.spot("added2", half, 0, sign)
            self.add(("far2", half, 0, sign), slot, rows_of)
            self.send("added2", half, 0, sign)

    def finish(self):
        for kind in ("plain2", "added2"):
            for half in (0, 1):
                for sign in (1, -1):
                    _, rows_of = self.spot(kind, half, 0, sign)
                    self.add((kind, half, 0, sign), self.place, rows_of)

    def drain(self):
        for key in self.keys:
            self.copy(*key).wait_send()


PAIRS = (
    ((2, 2), (2, -1)),
    ((-1, 2), (2, 1)),
    ((1, 2), (2, 0)),
    ((0, 2), (-1, -1)),
    ((1, -1), (-1, 1)),
    ((1, 1), (-1, 0)),
    ((0, -1), (1, 0)),
    ((0, 1), (0, 0)),
)


def pair_slot(place, step, member):
    dx, dy = 0, 0
    for k, pair in enumerate(PAIRS):
        dx = jnp.where(step == k, pair[member][0], dx)
        dy = jnp.where(step == k, pair[member][1], dy)
    return place_of(place, dx, dy)


def experts_kernel(
    x_ref, gates_ref, wg_hbm, wu_hbm, wd_hbm, hidden_ref, out_ref, parts, land, held, wg_ref, wu_ref, wd_ref,
    sends, receives, load_sems, weight_sems,
):
    place = lax.axis_index("tok")
    rows = parts.shape[1]

    def load(step, side, member):
        return pltpu.make_async_copy(
            x_ref.at[pair_slot(place, step, member)],
            held.at[side, pl.ds(member * rows, rows)],
            load_sems.at[side, member],
        )

    def weight(kind, e):
        src, dst = ((wg_hbm, wg_ref), (wu_hbm, wu_ref), (wd_hbm, wd_ref))[kind]
        return pltpu.make_async_copy(src.at[e], dst.at[e], weight_sems.at[kind, e])

    for member in (0, 1):
        load(0, 0, member).start()
    for e in range(wg_ref.shape[0]):
        for kind in range(3):
            weight(kind, e).start()
    greet(torus_peers())
    back = TorusScatter(parts, land, rows, sends, receives)

    @pl.loop(0, len(PAIRS))
    def _(step):
        side = step % 2
        for member in (0, 1):
            load(step, side, member).wait()

        @pl.when(step < len(PAIRS) - 1)
        def _():
            for member in (0, 1):
                load(step + 1, 1 - side, member).start()

        slots = [pair_slot(place, step, member) for member in (0, 1)]
        gates = jnp.concatenate([gates_ref[s].T for s in slots], axis=0)
        x = held[side]
        total = jnp.zeros((2 * rows, wd_ref.shape[2]), F32)
        for e in range(wg_ref.shape[0]):

            @pl.when(step == 0)
            def _():
                for kind in range(3):
                    weight(kind, e).wait()

            g = jnp.dot(x, wg_ref[e], preferred_element_type=F32)
            u = jnp.dot(x, wu_ref[e], preferred_element_type=F32)
            act = (g / (1.0 + jnp.exp(-g)) * u).astype(BF)
            o = jnp.dot(act, wd_ref[e], preferred_element_type=F32).astype(BF).astype(F32)
            total = total + gates[:, e : e + 1] * o
        for member in (0, 1):
            parts[slots[member]] = total[member * rows : (member + 1) * rows].astype(BF)
        for k, pair in enumerate(PAIRS):

            @pl.when(step == k)
            def _():
                for unit in pair:
                    back.send_unit(*unit)
                if k == 3:
                    for half in (0, 1):
                        back.pass_on(half, 2)
                if k == 5:
                    for half in (0, 1):
                        for a in (-1, 1):
                            back.pass_on(half, a)
                    for half in (0, 1):
                        back.complete(half, 2)

    for half in (0, 1):
        back.pass_on(half, 0)
    for half in (0, 1):
        for a in (-1, 1):
            back.complete(half, a)
    for half in (0, 1):
        back.pass_on_last(half)
    for half in (0, 1):
        back.complete(half, 0)
    back.finish()
    back.drain()
    out_ref[...] = (hidden_ref[...] + parts[place].astype(F32)).astype(out_ref.dtype)


def run_experts(x, gates, w_gate, w_up, w_down, hidden, collective_id):
    count = len(scatter_messages())
    _, rows, width = x.shape
    dma = pltpu.SemaphoreType.DMA
    vmem, anywhere = pl.BlockSpec(memory_space=pltpu.VMEM), pl.BlockSpec(memory_space=pl.ANY)
    return pl.pallas_call(
        experts_kernel,
        in_specs=[anywhere, vmem] + [anywhere] * 3 + [vmem],
        out_specs=vmem,
        out_shape=jax.ShapeDtypeStruct((rows, width), x.dtype),
        scratch_shapes=[
            pltpu.VMEM(x.shape, x.dtype),
            pltpu.VMEM((count, rows // 4, width), x.dtype),
            pltpu.VMEM((2, 2 * rows, width), x.dtype),
            pltpu.VMEM(w_gate.shape, w_gate.dtype),
            pltpu.VMEM(w_up.shape, w_up.dtype),
            pltpu.VMEM(w_down.shape, w_down.dtype),
            dma((count,)),
            dma((count,)),
            dma((2, 2)),
            dma((3, w_gate.shape[0])),
        ],
        compiler_params=pltpu.CompilerParams(
            collective_id=collective_id, has_side_effects=True, vmem_limit_bytes=VMEM_CAP
        ),
        name="experts",
    )(x, gates, w_gate, w_up, w_down, hidden)


def ring_messages(kinds):
    return {key: i for i, key in enumerate(kinds)}


GATHER_RING = ring_messages(
    [("near", 1), ("near", -1), ("rest", 1), ("rest", -1), ("far", 1), ("far", -1), ("pair", 0), ("pair", 1), ("pair", -1), ("half", 1), ("half", -1)]
)
SCATTER_RING = ring_messages(
    [("pair", 2), ("pair", 1), ("pair", -1), ("pair", 0)]
    + [(kind, sign) for kind in ("far", "plain", "added") for sign in (1, -1)]
)


def head_of(head, dz, flip=0):
    core = head % 2
    return ((head // 2 + dz + 4) % 4) * 2 + (core + flip) % 2


def ring_peers():
    place, head = lax.axis_index("tok"), lax.axis_index("head")
    return [(place, head_of(head, 1)), (place, head_of(head, -1)), (place, head_of(head, 0, 1))]


def ring_gather(own, out, rows, sends, receives, keys):
    place, head = lax.axis_index("tok"), lax.axis_index("head")
    started = []

    def copy(key, landing=False):
        kind, value = key
        begin, size = 0, rows
        if kind in ("near", "rest", "far", "half"):
            size = rows // 2
            begin = size if (value == 1) == (kind == "rest") else 0
        dz = {"near": 0, "rest": 0, "far": -value, "pair": value, "half": 2}[kind]
        crossing = kind in ("pair", "half")
        if landing:
            slot = head_of(head, dz, 1) if crossing else head_of(head, dz - value)
        else:
            slot = head_of(head, dz)
        target = out.at[slot, pl.ds(begin, size)]
        src = own.at[pl.ds(begin, size)] if not landing and dz == 0 else target
        peer = head_of(head, 0, 1) if crossing else head_of(head, value)
        return pltpu.make_async_remote_copy(
            src_ref=src,
            dst_ref=target,
            send_sem=sends.at[keys[key]],
            recv_sem=receives.at[keys[key]],
            device_id=(place, peer),
            device_id_type=MESH_ID,
        )

    def send(*key):
        c = copy(key)
        c.start()
        started.append(c)

    def arrive(*key):
        copy(key, landing=True).wait_recv()

    for kind in ("near", "rest"):
        send(kind, 1)
        send(kind, -1)
    send("pair", 0)
    yield
    arrive("pair", 0)
    yield
    for sign in (1, -1):
        arrive("near", sign)
        send("far", sign)
    for sign in (1, -1):
        arrive("rest", sign)
        send("pair", -sign)
    yield
    for dz in (1, -1):
        arrive("pair", dz)
    yield
    for sign in (1, -1):
        arrive("far", sign)
        send("half", sign)
    yield
    for sign in (1, -1):
        arrive("half", sign)
    for c in started:
        c.wait_send()
    yield


def opening_kernel(
    tokens_ref, gain_ref, cache_ref, gates_ref, wq_ref, wkv_ref, angles_ref, q_ref, near_ref, cache_out, gates_out,
    x_ref, gathered, cos_ref, sin_ref, ts, tr, hs, hr, gs, gr, ks, kr, own_sems,
):
    place, head = lax.axis_index("tok"), lax.axis_index("head")
    count = gates_ref.shape[0]
    rows = x_ref.shape[0]
    row_len = near_ref.shape[0] // 2
    heads = q_ref.shape[0]
    others = [((place + d) % count, head) for d in range(1, count)]
    x_ref[...] = rms_scale(tokens_ref[...], gain_ref[...].reshape(1, -1)).astype(x_ref.dtype)
    greet(others + ring_peers())
    mine = [
        pltpu.make_async_copy(cache_ref, cache_out.at[place], own_sems.at[0]),
        pltpu.make_async_copy(gates_ref.at[place], gates_out.at[place], own_sems.at[1]),
    ]
    one = ring_gather(x_ref, gathered, rows, hs, hr, GATHER_RING)
    two = torus_gather(cache_ref, cache_out, cache_ref.shape[0], ts, tr, torus_messages())

    def gate_copy(d, landing=False):
        target = (place + d) % count
        slot = (place - d + count) % count if landing else place
        return pltpu.make_async_remote_copy(
            src_ref=gates_ref.at[target],
            dst_ref=gates_out.at[slot],
            send_sem=gs.at[d],
            recv_sem=gr.at[d],
            device_id=(target, head),
            device_id_type=MESH_ID,
        )

    def onward(block):
        at = pl.multiple_of(block * rows, rows)
        return pltpu.make_async_remote_copy(
            src_ref=near_ref.at[pl.ds(row_len + at, rows)],
            dst_ref=near_ref.at[pl.ds(at, rows)],
            send_sem=ks.at[block],
            recv_sem=kr.at[block],
            device_id=((place + 1) % count, head),
            device_id_type=MESH_ID,
        )

    def project(block, x):
        at = pl.multiple_of(block * rows, rows)
        here = pl.ds(at, rows)
        turned = turn(x, wq_ref[...], wkv_ref[...], cos_ref[here], sin_ref[here])
        pad = jnp.zeros((rows, HS), BF)
        for h in range(heads):
            q_ref[h, here] = jnp.concatenate([turned[:, h * HS : (h + 1) * HS], pad], axis=1)
        near_ref[pl.ds(row_len + at, rows)] = turned[:, heads * HS :]
        onward(block).start()

    next(one)
    next(two)
    for c in mine:
        c.start()
    for d in range(1, count):
        gate_copy(d).start()
    half = HS // 2
    cos, sin = angles_ref[:half].T, angles_ref[half:].T
    cos_ref[...] = jnp.concatenate([cos] * 4, axis=1)
    sin_ref[...] = jnp.concatenate([sin] * 4, axis=1)

    def project_slots(*slots):
        for block in slots:
            project(block, gathered[block])

    project(head, x_ref[...])
    next(two)
    next(one)
    project_slots(head_of(head, 0, 1))
    next(two)
    next(two)
    next(one)
    project_slots(head_of(head, 1), head_of(head, -1))
    next(one)
    project_slots(head_of(head, 1, 1), head_of(head, -1, 1))
    next(two)
    next(two)
    next(one)
    project_slots(head_of(head, 2))
    next(two)
    next(one)
    project_slots(head_of(head, 2, 1))
    for _ in two:
        pass
    for d in range(1, count):
        gate_copy(d, True).wait_recv()
    for d in range(1, count):
        gate_copy(d).wait_send()
    for c in mine:
        c.wait()
    for dz in range(4):
        for flip in (0, 1):
            onward(head_of(head, dz, flip)).wait_recv()
    for dz in range(4):
        for flip in (0, 1):
            onward(head_of(head, dz, flip)).wait_send()


def opening(x, gain, cache, gates, w_query, w_keyval, angles, collective_id):
    t, r, n = len(torus_messages()), len(GATHER_RING), gates.shape[0]
    rows, width = x.shape
    length = angles.shape[1]
    heads = w_query.shape[0] // HS
    dma = pltpu.SemaphoreType.DMA
    vmem, anywhere = pl.BlockSpec(memory_space=pltpu.VMEM), pl.BlockSpec(memory_space=pl.ANY)
    return pl.pallas_call(
        opening_kernel,
        in_specs=[vmem] * 7,
        out_specs=[vmem, vmem, anywhere, anywhere],
        out_shape=[
            jax.ShapeDtypeStruct((heads, length, 128), BF),
            jax.ShapeDtypeStruct((2 * length, 128), BF),
            jax.ShapeDtypeStruct((n,) + cache.shape, cache.dtype),
            jax.ShapeDtypeStruct(gates.shape, gates.dtype),
        ],
        scratch_shapes=[
            pltpu.VMEM((rows, width), BF),
            pltpu.VMEM((length // rows, rows, width), BF),
            pltpu.VMEM((length, 128), F32),
            pltpu.VMEM((length, 128), F32),
            dma((t,)),
            dma((t,)),
            dma((r,)),
            dma((r,)),
            dma((n,)),
            dma((n,)),
            dma((length // rows,)),
            dma((length // rows,)),
            dma((2,)),
        ],
        compiler_params=pltpu.CompilerParams(
            collective_id=collective_id, has_side_effects=True, vmem_limit_bytes=VMEM_CAP
        ),
        name="opening",
    )(x, gain, cache, gates, w_query, w_keyval, angles)


def ring_scatter(parts, pair_land, land, rows, sends, receives, keys):
    place, head = lax.axis_index("tok"), lax.axis_index("head")
    started = []
    low, high = pl.ds(0, rows // 2), pl.ds(rows // 2, rows // 2)

    def spot(key):
        kind, value = key
        if kind == "far":
            return head_of(head, 2), (low if value == 1 else high)
        if kind == "plain":
            return head_of(head, value), (high if value == 1 else low)
        return head_of(head, value), (low if value == 1 else high)

    def copy(key):
        kind, value = key
        if kind == "pair":
            src, dst = parts.at[head_of(head, value, 1)], pair_land.at[keys[key]]
            peer = head_of(head, 0, 1)
        else:
            slot, rows_of = spot(key)
            src, dst = parts.at[slot, rows_of], land.at[keys[key] - 4]
            peer = head_of(head, value)
        return pltpu.make_async_remote_copy(
            src_ref=src,
            dst_ref=dst,
            send_sem=sends.at[keys[key]],
            recv_sem=receives.at[keys[key]],
            device_id=(place, peer),
            device_id_type=MESH_ID,
        )

    def send(*key):
        c = copy(key)
        c.start()
        started.append(c)

    def add(key, slot, rows_of, buffer, index):
        copy(key).wait_recv()
        parts[slot, rows_of] = (parts[slot, rows_of].astype(F32) + buffer[index].astype(F32)).astype(parts.dtype)

    def add_pair(dz):
        key = ("pair", dz)
        add(key, head_of(head, dz), pl.ds(0, rows), pair_land, keys[key])

    for dz in (2, 1, -1, 0):
        send("pair", dz)
    add_pair(2)
    for sign in (1, -1):
        send("far", sign)
    for sign in (1, -1):
        add_pair(sign)
        send("plain", sign)
    add_pair(0)
    for sign in (1, -1):
        key = ("far", sign)
        slot, rows_of = spot(("added", sign))
        add(key, slot, rows_of, land, keys[key] - 4)
        send("added", sign)
    for kind in ("plain", "added"):
        for sign in (1, -1):
            key = (kind, sign)
            _, rows_of = spot(key)
            add(key, head, rows_of, land, keys[key] - 4)
    for c in started:
        c.wait_send()


def settle_kernel(
    part_ref, tokens_ref, gain_ref, hidden_ref, out_ref, parts, pair_land, land, normed, rs, rr, ts, tr, own_sems
):
    place, head = lax.axis_index("tok"), lax.axis_index("head")
    rows = tokens_ref.shape[0]
    loads = [
        pltpu.make_async_copy(part_ref.at[pl.ds(h * rows, rows)], parts.at[h], own_sems.at[h]) for h in range(8)
    ]
    for c in loads:
        c.start()
    greet(torus_peers() + ring_peers())
    for c in loads:
        c.wait()
    ring_scatter(parts, pair_land, land, rows, rs, rr, SCATTER_RING)
    hidden = tokens_ref[...].astype(F32) + parts[head].astype(F32)
    hidden_ref[...] = hidden
    normed[...] = rms_scale(hidden, gain_ref[...].reshape(1, -1)).astype(normed.dtype)
    mine = pltpu.make_async_copy(normed, out_ref.at[place], own_sems.at[8])
    mine.start()
    for _ in torus_gather(normed, out_ref, rows, ts, tr, torus_messages()):
        pass
    mine.wait()


def settle(partial, tokens, gain, collective_id):
    rows, width = tokens.shape
    t, r = len(torus_messages()), len(SCATTER_RING)
    dma = pltpu.SemaphoreType.DMA
    return pl.pallas_call(
        settle_kernel,
        in_specs=[
            pl.BlockSpec(memory_space=pl.ANY),
            pl.BlockSpec(memory_space=pltpu.VMEM),
            pl.BlockSpec(memory_space=pltpu.VMEM),
        ],
        out_specs=[pl.BlockSpec(memory_space=pltpu.VMEM), pl.BlockSpec(memory_space=pl.ANY)],
        out_shape=[
            jax.ShapeDtypeStruct((rows, width), F32),
            jax.ShapeDtypeStruct((16, rows, width), BF),
        ],
        scratch_shapes=[
            pltpu.VMEM((8, rows, width), BF),
            pltpu.VMEM((4, rows, width), BF),
            pltpu.VMEM((6, rows // 2, width), BF),
            pltpu.VMEM((rows, width), BF),
            dma((r,)),
            dma((r,)),
            dma((t,)),
            dma((t,)),
            dma((9,)),
        ],
        compiler_params=pltpu.CompilerParams(
            collective_id=collective_id, has_side_effects=True, vmem_limit_bytes=VMEM_CAP
        ),
        name="settle",
    )(partial, tokens, gain)


def local(
    tokens,
    segments,
    group_ids,
    prefix_owner,
    slab_fill,
    prefix_cache,
    attn_gain,
    w_query,
    w_keyval,
    w_out,
    ffn_gain,
    routes,
    route_gates,
    w_gate,
    w_up,
    w_down,
):
    tok_count = lax.axis_size("tok")
    head_count = lax.axis_size("head")
    place = lax.axis_index("tok")
    row_len = tokens.shape[0] * head_count
    exp_local = w_gate.shape[0]
    experts = jnp.arange(EXPERTS, dtype=jnp.int32)[:, None, None]
    gates = jnp.sum(jnp.where(routes.T[None] == experts, route_gates.T[None], 0.0), axis=1)
    gates = gates.reshape(tok_count, exp_local, -1)
    gates = jnp.concatenate([gates, jnp.zeros((tok_count, 8 - exp_local, gates.shape[2]), F32)], axis=1)

    padded = jnp.concatenate([jnp.full((row_len,), -1, jnp.int32), segments])
    window = lax.dynamic_slice_in_dim(padded, place * row_len, 2 * row_len, 0)
    own = window[row_len:]
    begins, slabs, fills = request_tables(window, own, group_ids, prefix_owner, slab_fill)
    positions = fills + row_len + jnp.arange(row_len, dtype=jnp.int32) - begins
    steps_idx = jnp.arange(HS // 2, dtype=F32)
    inverse = jnp.exp(steps_idx * (-2.0 * jnp.log(10000.0) / HS))
    angles = inverse[:, None] * positions.astype(F32)[None, :]
    turns = jnp.concatenate([jnp.cos(angles), jnp.sin(angles)], axis=0)
    q, near, cache, gates_all = opening(tokens, attn_gain, prefix_cache, gates, w_query.T, w_keyval, turns, 1)
    cache = cache.reshape(-1, cache.shape[-1])

    span = 128
    blocks = row_len // span
    first_begin = begins.reshape(blocks, span)[:, 0]
    ends = row_len + jnp.arange(blocks, dtype=jnp.int32) * span
    steps = jnp.maximum(ends - first_begin + 2 * span - 1, 0) // (2 * span)
    ids = jnp.arange(tok_count, dtype=jnp.int32)
    present = jnp.max((slabs.reshape(blocks, span)[:, :, None] == ids).astype(jnp.int32), axis=1)
    earlier = jnp.sum(jnp.where(ids[:, None] < ids[None, :], present[:, :, None], 0), axis=1)
    listed = (present[:, None, :] == 1) & (earlier[:, None, :] == ids[None, :, None])
    used = jnp.sum(jnp.where(listed, ids, 0), axis=2)
    used = jnp.concatenate([jnp.sum(present, axis=1, keepdims=True), used], axis=1)
    rows = jnp.concatenate([begins[None], slabs[None], jnp.zeros((6, row_len), jnp.int32)], axis=0)

    partial = attend(q, near, cache, rows, steps, used, slab_fill, w_out)
    hidden, arrived = settle(partial, tokens, ffn_gain, 2)
    return run_experts(arrived, gates_all, w_gate, w_up, w_down, hidden, 3)


def solution(mesh):
    return jax.shard_map(
        local,
        mesh=mesh,
        in_specs=(
            P(("tok", "head"), None),
            P(),
            P(),
            P(),
            P(),
            P("tok", "head"),
            P(),
            P(None, "head"),
            P(None, "head"),
            P("head", None),
            P(),
            P(("tok", "head"), None),
            P(("tok", "head"), None),
            P("tok", None, None),
            P("tok", None, None),
            P("tok", None, None),
        ),
        out_specs=P(("tok", "head"), None),
        check_vma=False,
    )
```

```python
import functools

import jax
import jax.numpy as jnp
from jax import lax
from jax.experimental import pallas as pl
from jax.experimental.pallas import tpu as pltpu
from jax.sharding import PartitionSpec as P

HS = 64
EXPERTS = 32
TOPK = 8
PREFIX = 512
NEG_FILL = -1e30
NORM_EPS = 1e-06
LOG2E = 1.4426950408889634
BF = jnp.bfloat16
F32 = jnp.float32
VMEM_CAP = 60 * 1024 * 1024


def rms_scale(values, gain):
    widened = values.astype(F32)
    spread = jnp.mean(widened * widened, axis=-1, keepdims=True)
    return widened * lax.rsqrt(spread + NORM_EPS) * gain


def request_tables(window, own, group_ids, prefix_owner, slab_fill):
    reqs = group_ids.shape[0]
    ids = jnp.arange(reqs, dtype=jnp.int32)
    slabs = jnp.arange(prefix_owner.shape[0], dtype=jnp.int32)
    begins = jnp.sum((window[None, :] < ids[:, None]).astype(jnp.int32), axis=1)
    slab_of = jnp.sum(jnp.where(group_ids[:, None] == slabs, prefix_owner, 0), axis=1)
    fill_of = jnp.sum(jnp.where(slab_of[:, None] == slabs, slab_fill, 0), axis=1)
    packed = (begins * 16 + slab_of) * 1024 + fill_of
    mine = jnp.sum(jnp.where(own[None, :] == ids[:, None], packed[:, None], 0), axis=0)
    return mine // (16 * 1024), (mine // 1024) % 16, mine % 1024


def turn(x, wq, wkv, cos, sin):
    both = jnp.concatenate(
        [
            lax.dot_general(x, wq, (((1,), (1,)), ((), ())), preferred_element_type=F32),
            jnp.dot(x, wkv, preferred_element_type=F32),
        ],
        axis=1,
    )
    width = both.shape[1]
    lane = lax.broadcasted_iota(jnp.int32, both.shape, 1)
    swapped = jnp.where(
        lane % HS < HS // 2,
        -pltpu.roll(both, width - HS // 2, 1),
        pltpu.roll(both, HS // 2, 1),
    )
    copies = -(-width // 128)
    cos = jnp.concatenate([cos] * copies, axis=1)[:, :width]
    sin = jnp.concatenate([sin] * copies, axis=1)[:, :width]
    return jnp.where(lane < wq.shape[0] + HS, both * cos + swapped * sin, both).astype(BF)


def attend_kernel(
    steps_ref, used_ref, fill_ref, q_ref, near_ref, cache_ref, rows_ref, wout_ref, out_ref
):
    block = pl.program_id(0)
    heads, span = q_ref.shape[0], q_ref.shape[1]
    row_len = near_ref.shape[0] // 2
    scale = HS ** (-0.5) * LOG2E

    queries = jnp.concatenate([q_ref[h] for h in range(heads)], axis=0)
    begins = jnp.concatenate([rows_ref[0:1]] * heads, axis=1)
    slabs = jnp.concatenate([rows_ref[1:2]] * heads, axis=1)
    offset = row_len + block * span
    wide = heads * span

    def scores(kv):
        return lax.dot_general(kv, queries, (((1,), (1,)), ((), ())), preferred_element_type=F32)

    def absorb(blocks, carry):
        peak, total, acc = carry
        peak_new = peak
        for s, _ in blocks:
            peak_new = jnp.maximum(peak_new, jnp.max(s, axis=0, keepdims=True))
        factor = jnp.exp2((peak - peak_new) * scale)
        total, acc = total * factor, acc * factor
        for s, kv in blocks:
            weights = jnp.exp2((s - peak_new) * scale)
            total = total + jnp.sum(weights, axis=0, keepdims=True)
            acc = acc + jnp.dot(kv.T[HS:], weights.astype(BF), preferred_element_type=F32)
        return peak_new, total, acc

    def own():
        kv = near_ref[pl.ds(pl.multiple_of(offset, span), span)]
        key = lax.broadcasted_iota(jnp.int32, (span, wide), 0)
        query = lax.broadcasted_iota(jnp.int32, (span, wide), 1) % span
        return jnp.where((key <= query) & (key >= begins - offset), scores(kv), NEG_FILL), kv

    chunk = 2 * span

    def near(step):
        first = pl.multiple_of(offset - (step + 1) * chunk, span)
        kv = near_ref[pl.ds(first, chunk)]
        key = lax.broadcasted_iota(jnp.int32, (chunk, wide), 0)
        return jnp.where(key >= begins - first, scores(kv), NEG_FILL), kv

    def far(step):
        slab = used_ref[block, step + 1]
        kv = cache_ref[pl.ds(pl.multiple_of(slab * PREFIX, PREFIX), PREFIX)]
        key = lax.broadcasted_iota(jnp.int32, (PREFIX, wide), 0)
        limit = jnp.where(slabs == slab, fill_ref[slab], 0)
        return jnp.where(key < limit, scores(kv), NEG_FILL), kv

    def sweep(piece, start, count, carry):
        pairs = count // 2
        carry = lax.fori_loop(
            0, pairs, lambda i, c: absorb([piece(start + 2 * i), piece(start + 2 * i + 1)], c), carry
        )
        return lax.fori_loop(2 * pairs, count, lambda i, c: absorb([piece(start + i)], c), carry)

    carry = (
        jnp.full((1, wide), NEG_FILL, F32),
        jnp.zeros((1, wide), F32),
        jnp.zeros((HS, wide), F32),
    )
    carry = absorb([own(), far(0)], carry)
    carry = sweep(near, 0, steps_ref[block], carry)
    _, total, acc = sweep(far, 1, used_ref[block, 0] - 1, carry)
    mixed = (acc / total).T
    mixed = jnp.concatenate([mixed[h * span : (h + 1) * span] for h in range(heads)], axis=1)
    out_ref[...] = jnp.dot(mixed.astype(BF), wout_ref[...], preferred_element_type=F32).astype(BF)


def attend(q, near, cache, rows, steps, used, fill, w_out, span=128):
    heads, length, _ = q.shape
    whole = lambda a: pl.BlockSpec(a.shape, lambda i, *_: (0,) * a.ndim)
    return pl.pallas_call(
        attend_kernel,
        grid_spec=pltpu.PrefetchScalarGridSpec(
            num_scalar_prefetch=3,
            grid=(length // span,),
            in_specs=[
                pl.BlockSpec((heads, span, 128), lambda i, *_: (0, i, 0)),
                whole(near),
                whole(cache),
                pl.BlockSpec((8, span), lambda i, *_: (0, i)),
                whole(w_out),
            ],
            out_specs=pl.BlockSpec((span, w_out.shape[1]), lambda i, *_: (i, 0)),
        ),
        out_shape=jax.ShapeDtypeStruct((length, w_out.shape[1]), BF),
        compiler_params=pltpu.CompilerParams(vmem_limit_bytes=VMEM_CAP),
        name="attend",
    )(steps, used, fill, q, near, cache, rows, w_out)


MESH_ID = pl.DeviceIdType.MESH


def torus_messages():
    keys = []
    for half in (0, 1):
        for sign in (1, -1):
            keys.append(("near", half, 0, sign))
            keys.append(("far", half, 0, sign))
            for a in (0, -1, 1, 2):
                keys.append(("side", half, a, sign))
                keys.append(("last", half, a, sign))
    return {key: i for i, key in enumerate(keys)}


def place_of(place, dx, dy):
    return ((place // 4 + dx + 4) % 4) * 4 + (place % 4 + dy + 4) % 4


def torus_gather(own, out, rows, sends, receives, keys):
    place, head = lax.axis_index("tok"), lax.axis_index("head")
    half_rows, part = rows // 2, rows // 4
    started = []

    def unit(half, a, b):
        return (a, b) if half == 0 else (b, a)

    def copy(key, landing=False):
        kind, half, a, sign = key
        first = kind in ("near", "far")
        if kind == "near":
            source = (0, 0)
        elif kind == "far":
            source = (-sign, 0)
        elif kind == "side":
            source = (a, 0)
        else:
            source = (a, -sign)
        begin, size = half * half_rows, half_rows
        if kind in ("far", "last"):
            begin, size = begin + (0 if sign == 1 else part), part
        if landing:
            source = (source[0] - sign, source[1]) if first else (source[0], source[1] - sign)
        slot = place_of(place, *unit(half, *source))
        step = unit(half, sign, 0) if first else unit(half, 0, sign)
        target = out.at[slot, pl.ds(begin, size)]
        if not landing and source == (0, 0):
            src = own.at[pl.ds(begin, size)]
        else:
            src = target
        return pltpu.make_async_remote_copy(
            src_ref=src,
            dst_ref=target,
            send_sem=sends.at[keys[key]],
            recv_sem=receives.at[keys[key]],
            device_id=(place_of(place, *step), head),
            device_id_type=MESH_ID,
        )

    def send(*key):
        c = copy(key)
        c.start()
        started.append(c)

    def arrive(*key):
        copy(key, landing=True).wait_recv()

    for sign in (1, -1):
        for half in (0, 1):
            send("near", half, 0, sign)
    for sign in (1, -1):
        for half in (0, 1):
            send("side", half, 0, sign)
    yield
    for sign in (1, -1):
        for half in (0, 1):
            arrive("near", half, 0, sign)
            send("far", half, 0, sign)
            send("side", half, -sign, 1)
            send("side", half, -sign, -1)
    yield
    for sign in (1, -1):
        for half in (0, 1):
            arrive("side", half, 0, sign)
            send("last", half, 0, sign)
    yield
    for half in (0, 1):
        for sign in (1, -1):
            arrive("far", half, 0, sign)
        for sign in (1, -1):
            send("side", half, 2, sign)
    yield
    for a in (-1, 1, 2):
        for sign in (1, -1):
            for half in (0, 1):
                arrive("side", half, a, sign)
                send("last", half, a, sign)
        yield
    for a in (0, -1, 1, 2):
        for half in (0, 1):
            for sign in (1, -1):
                arrive("last", half, a, sign)
    for c in started:
        c.wait_send()
    yield


def greet(peers):
    barrier = pltpu.get_barrier_semaphore()
    for peer in peers:
        pl.semaphore_signal(barrier, inc=1, device_id=peer, device_id_type=MESH_ID)
    pl.semaphore_wait(barrier, len(peers))


def torus_peers():
    place, head = lax.axis_index("tok"), lax.axis_index("head")
    return [(place_of(place, *s), head) for s in ((1, 0), (-1, 0), (0, 1), (0, -1))]


def scatter_messages():
    keys = []
    for half in (0, 1):
        for a in (2, -1, 1, 0):
            for sign in (1, -1):
                for kind in ("far", "plain", "added"):
                    keys.append((kind, half, a, sign))
        for sign in (1, -1):
            for kind in ("far2", "plain2", "added2"):
                keys.append((kind, half, 0, sign))
    return {key: i for i, key in enumerate(keys)}


class TorusScatter:
    def __init__(self, parts, land, rows, sends, receives):
        self.parts, self.land, self.sends, self.receives = parts, land, sends, receives
        self.keys = scatter_messages()
        self.rows = rows
        self.place, self.head = lax.axis_index("tok"), lax.axis_index("head")

    def slot(self, half, a, b):
        return place_of(self.place, *((a, b) if half == 0 else (b, a)))

    def spot(self, kind, half, a, sign):
        base, part = half * self.rows // 2, self.rows // 4
        low, high = pl.ds(base, part), pl.ds(base + part, part)
        with_far, plain = (low, high) if sign == 1 else (high, low)
        distance = 2 if kind.startswith("far") else sign
        offset = (distance, 0) if kind.endswith("2") else (a, distance)
        return self.slot(half, *offset), plain if kind.startswith("plain") else with_far

    def copy(self, *key):
        kind, half, a, sign = key
        slot, rows_of = self.spot(*key)
        step = (sign, 0) if kind.endswith("2") else (0, sign)
        return pltpu.make_async_remote_copy(
            src_ref=self.parts.at[slot, rows_of],
            dst_ref=self.land.at[self.keys[key]],
            send_sem=self.sends.at[self.keys[key]],
            recv_sem=self.receives.at[self.keys[key]],
            device_id=(self.slot(half, *step), self.head),
            device_id_type=MESH_ID,
        )

    def send(self, *key):
        self.copy(*key).start()

    def add(self, key, slot, rows_of):
        self.copy(*key).wait_recv()
        self.parts[slot, rows_of] = (
            self.parts[slot, rows_of].astype(F32) + self.land[self.keys[key]].astype(F32)
        ).astype(self.parts.dtype)

    def send_unit(self, dx, dy):
        for half, a, b in ((0, dx, dy), (1, dy, dx)):
            if b == 2:
                self.send("far", half, a, 1)
                self.send("far", half, a, -1)
            elif b != 0:
                self.send("plain", half, a, b)

    def pass_on(self, half, a):
        for sign in (1, -1):
            slot, rows_of = self.spot("added", half, a, sign)
            self.add(("far", half, a, sign), slot, rows_of)
            self.send("added", half, a, sign)

    def complete(self, half, a):
        slot = self.slot(half, a, 0)
        for sign in (1, -1):
            for kind in ("plain", "added"):
                _, rows_of = self.spot(kind, half, a, sign)
                self.add((kind, half, a, sign), slot, rows_of)
        if a == 2:
            self.send("far2", half, 0, 1)
            self.send("far2", half, 0, -1)
        elif a != 0:
            self.send("plain2", half, 0, a)

    def pass_on_last(self, half):
        for sign in (1, -1):
            slot, rows_of = self.spot("added2", half, 0, sign)
            self.add(("far2", half, 0, sign), slot, rows_of)
            self.send("added2", half, 0, sign)

    def finish(self):
        for kind in ("plain2", "added2"):
            for half in (0, 1):
                for sign in (1, -1):
                    _, rows_of = self.spot(kind, half, 0, sign)
                    self.add((kind, half, 0, sign), self.place, rows_of)

    def drain(self):
        for key in self.keys:
            self.copy(*key).wait_send()


PAIRS = (
    ((2, 2), (2, -1)),
    ((-1, 2), (2, 1)),
    ((1, 2), (2, 0)),
    ((0, 2), (-1, -1)),
    ((1, -1), (-1, 1)),
    ((1, 1), (-1, 0)),
    ((0, -1), (1, 0)),
    ((0, 1), (0, 0)),
)


def pair_slot(place, step, member):
    dx, dy = 0, 0
    for k, pair in enumerate(PAIRS):
        dx = jnp.where(step == k, pair[member][0], dx)
        dy = jnp.where(step == k, pair[member][1], dy)
    return place_of(place, dx, dy)


def experts_kernel(
    x_ref, gates_ref, wg_hbm, wu_hbm, wd_hbm, hidden_ref, out_ref, parts, land, held, wg_ref, wu_ref, wd_ref,
    sends, receives, load_sems, weight_sems,
):
    place = lax.axis_index("tok")
    rows = parts.shape[1]

    def load(step, side, member):
        return pltpu.make_async_copy(
            x_ref.at[pair_slot(place, step, member)],
            held.at[side, pl.ds(member * rows, rows)],
            load_sems.at[side, member],
        )

    def weight(kind, e):
        src, dst = ((wg_hbm, wg_ref), (wu_hbm, wu_ref), (wd_hbm, wd_ref))[kind]
        return pltpu.make_async_copy(src.at[e], dst.at[e], weight_sems.at[kind, e])

    for member in (0, 1):
        load(0, 0, member).start()
    for e in range(wg_ref.shape[0]):
        for kind in range(3):
            weight(kind, e).start()
    greet(torus_peers())
    back = TorusScatter(parts, land, rows, sends, receives)

    @pl.loop(0, len(PAIRS))
    def _(step):
        side = step % 2
        for member in (0, 1):
            load(step, side, member).wait()

        @pl.when(step < len(PAIRS) - 1)
        def _():
            for member in (0, 1):
                load(step + 1, 1 - side, member).start()

        slots = [pair_slot(place, step, member) for member in (0, 1)]
        gates = jnp.concatenate([gates_ref[s].T for s in slots], axis=0)
        x = held[side]
        total = jnp.zeros((2 * rows, wd_ref.shape[2]), F32)
        for e in range(wg_ref.shape[0]):

            @pl.when(step == 0)
            def _():
                for kind in range(3):
                    weight(kind, e).wait()

            g = jnp.dot(x, wg_ref[e], preferred_element_type=F32)
            u = jnp.dot(x, wu_ref[e], preferred_element_type=F32)
            act = (g / (1.0 + jnp.exp(-g)) * u).astype(BF)
            o = jnp.dot(act, wd_ref[e], preferred_element_type=F32).astype(BF).astype(F32)
            total = total + gates[:, e : e + 1] * o
        for member in (0, 1):
            parts[slots[member]] = total[member * rows : (member + 1) * rows].astype(BF)
        for k, pair in enumerate(PAIRS):

            @pl.when(step == k)
            def _():
                for unit in pair:
                    back.send_unit(*unit)
                if k == 3:
                    for half in (0, 1):
                        back.pass_on(half, 2)
                if k == 5:
                    for half in (0, 1):
                        for a in (-1, 1):
                            back.pass_on(half, a)
                    for half in (0, 1):
                        back.complete(half, 2)

    for half in (0, 1):
        back.pass_on(half, 0)
    for half in (0, 1):
        for a in (-1, 1):
            back.complete(half, a)
    for half in (0, 1):
        back.pass_on_last(half)
    for half in (0, 1):
        back.complete(half, 0)
    back.finish()
    back.drain()
    out_ref[...] = (hidden_ref[...] + parts[place].astype(F32)).astype(out_ref.dtype)


def run_experts(x, gates, w_gate, w_up, w_down, hidden, collective_id):
    count = len(scatter_messages())
    _, rows, width = x.shape
    dma = pltpu.SemaphoreType.DMA
    vmem, anywhere = pl.BlockSpec(memory_space=pltpu.VMEM), pl.BlockSpec(memory_space=pl.ANY)
    return pl.pallas_call(
        experts_kernel,
        in_specs=[anywhere, vmem] + [anywhere] * 3 + [vmem],
        out_specs=vmem,
        out_shape=jax.ShapeDtypeStruct((rows, width), x.dtype),
        scratch_shapes=[
            pltpu.VMEM(x.shape, x.dtype),
            pltpu.VMEM((count, rows // 4, width), x.dtype),
            pltpu.VMEM((2, 2 * rows, width), x.dtype),
            pltpu.VMEM(w_gate.shape, w_gate.dtype),
            pltpu.VMEM(w_up.shape, w_up.dtype),
            pltpu.VMEM(w_down.shape, w_down.dtype),
            dma((count,)),
            dma((count,)),
            dma((2, 2)),
            dma((3, w_gate.shape[0])),
        ],
        compiler_params=pltpu.CompilerParams(
            collective_id=collective_id, has_side_effects=True, vmem_limit_bytes=VMEM_CAP
        ),
        name="experts",
    )(x, gates, w_gate, w_up, w_down, hidden)


def ring_messages(kinds):
    return {key: i for i, key in enumerate(kinds)}


GATHER_RING = ring_messages(
    [("near", 1), ("near", -1), ("rest", 1), ("rest", -1), ("far", 1), ("far", -1), ("pair", 0), ("pair", 1), ("pair", -1), ("half", 1), ("half", -1)]
)
SCATTER_RING = ring_messages(
    [("pair", 2), ("pair", 1), ("pair", -1), ("pair", 0)]
    + [(kind, sign) for kind in ("far", "plain", "added") for sign in (1, -1)]
)


def head_of(head, dz, flip=0):
    core = head % 2
    return ((head // 2 + dz + 4) % 4) * 2 + (core + flip) % 2


def ring_peers():
    place, head = lax.axis_index("tok"), lax.axis_index("head")
    return [(place, head_of(head, 1)), (place, head_of(head, -1)), (place, head_of(head, 0, 1))]


def ring_gather(own, out, rows, sends, receives, keys):
    place, head = lax.axis_index("tok"), lax.axis_index("head")
    started = []

    def copy(key, landing=False):
        kind, value = key
        begin, size = 0, rows
        if kind in ("near", "rest", "far", "half"):
            size = rows // 2
            begin = size if (value == 1) == (kind == "rest") else 0
        dz = {"near": 0, "rest": 0, "far": -value, "pair": value, "half": 2}[kind]
        crossing = kind in ("pair", "half")
        if landing:
            slot = head_of(head, dz, 1) if crossing else head_of(head, dz - value)
        else:
            slot = head_of(head, dz)
        target = out.at[slot, pl.ds(begin, size)]
        src = own.at[pl.ds(begin, size)] if not landing and dz == 0 else target
        peer = head_of(head, 0, 1) if crossing else head_of(head, value)
        return pltpu.make_async_remote_copy(
            src_ref=src,
            dst_ref=target,
            send_sem=sends.at[keys[key]],
            recv_sem=receives.at[keys[key]],
            device_id=(place, peer),
            device_id_type=MESH_ID,
        )

    def send(*key):
        c = copy(key)
        c.start()
        started.append(c)

    def arrive(*key):
        copy(key, landing=True).wait_recv()

    for kind in ("near", "rest"):
        send(kind, 1)
        send(kind, -1)
    send("pair", 0)
    yield
    arrive("pair", 0)
    yield
    for sign in (1, -1):
        arrive("near", sign)
        send("far", sign)
    for sign in (1, -1):
        arrive("rest", sign)
        send("pair", -sign)
    yield
    for dz in (1, -1):
        arrive("pair", dz)
    yield
    for sign in (1, -1):
        arrive("far", sign)
        send("half", sign)
    yield
    for sign in (1, -1):
        arrive("half", sign)
    for c in started:
        c.wait_send()
    yield


def opening_kernel(
    tokens_ref, gain_ref, cache_ref, gates_ref, wq_ref, wkv_ref, angles_ref, q_ref, near_ref, cache_out, gates_out,
    x_ref, gathered, cos_ref, sin_ref, ts, tr, hs, hr, gs, gr, ks, kr, own_sems,
):
    place, head = lax.axis_index("tok"), lax.axis_index("head")
    count = gates_ref.shape[0]
    rows = x_ref.shape[0]
    row_len = near_ref.shape[0] // 2
    heads = q_ref.shape[0]
    others = [((place + d) % count, head) for d in range(1, count)]
    x_ref[...] = rms_scale(tokens_ref[...], gain_ref[...].reshape(1, -1)).astype(x_ref.dtype)
    greet(others + ring_peers())
    mine = [
        pltpu.make_async_copy(cache_ref, cache_out.at[place], own_sems.at[0]),
        pltpu.make_async_copy(gates_ref.at[place], gates_out.at[place], own_sems.at[1]),
    ]
    one = ring_gather(x_ref, gathered, rows, hs, hr, GATHER_RING)
    two = torus_gather(cache_ref, cache_out, cache_ref.shape[0], ts, tr, torus_messages())

    def gate_copy(d, landing=False):
        target = (place + d) % count
        slot = (place - d + count) % count if landing else place
        return pltpu.make_async_remote_copy(
            src_ref=gates_ref.at[target],
            dst_ref=gates_out.at[slot],
            send_sem=gs.at[d],
            recv_sem=gr.at[d],
            device_id=(target, head),
            device_id_type=MESH_ID,
        )

    def onward(block):
        at = pl.multiple_of(block * rows, rows)
        return pltpu.make_async_remote_copy(
            src_ref=near_ref.at[pl.ds(row_len + at, rows)],
            dst_ref=near_ref.at[pl.ds(at, rows)],
            send_sem=ks.at[block],
            recv_sem=kr.at[block],
            device_id=((place + 1) % count, head),
            device_id_type=MESH_ID,
        )

    def project(block, x):
        at = pl.multiple_of(block * rows, rows)
        here = pl.ds(at, rows)
        turned = turn(x, wq_ref[...], wkv_ref[...], cos_ref[here], sin_ref[here])
        pad = jnp.zeros((rows, HS), BF)
        for h in range(heads):
            q_ref[h, here] = jnp.concatenate([turned[:, h * HS : (h + 1) * HS], pad], axis=1)
        near_ref[pl.ds(row_len + at, rows)] = turned[:, heads * HS :]
        onward(block).start()

    next(one)
    next(two)
    for c in mine:
        c.start()
    for d in range(1, count):
        gate_copy(d).start()
    half = HS // 2
    cos, sin = angles_ref[:half].T, angles_ref[half:].T
    cos_ref[...] = jnp.concatenate([cos] * 4, axis=1)
    sin_ref[...] = jnp.concatenate([sin] * 4, axis=1)

    def project_slots(*slots):
        for block in slots:
            project(block, gathered[block])

    project(head, x_ref[...])
    next(two)
    next(one)
    project_slots(head_of(head, 0, 1))
    next(two)
    next(two)
    next(one)
    project_slots(head_of(head, 1), head_of(head, -1))
    next(one)
    project_slots(head_of(head, 1, 1), head_of(head, -1, 1))
    next(two)
    next(two)
    next(one)
    project_slots(head_of(head, 2))
    next(two)
    next(one)
    project_slots(head_of(head, 2, 1))
    for _ in two:
        pass
    for d in range(1, count):
        gate_copy(d, True).wait_recv()
    for d in range(1, count):
        gate_copy(d).wait_send()
    for c in mine:
        c.wait()
    for dz in range(4):
        for flip in (0, 1):
            onward(head_of(head, dz, flip)).wait_recv()
    for dz in range(4):
        for flip in (0, 1):
            onward(head_of(head, dz, flip)).wait_send()


def opening(x, gain, cache, gates, w_query, w_keyval, angles, collective_id):
    t, r, n = len(torus_messages()), len(GATHER_RING), gates.shape[0]
    rows, width = x.shape
    length = angles.shape[1]
    heads = w_query.shape[0] // HS
    dma = pltpu.SemaphoreType.DMA
    vmem, anywhere = pl.BlockSpec(memory_space=pltpu.VMEM), pl.BlockSpec(memory_space=pl.ANY)
    return pl.pallas_call(
        opening_kernel,
        in_specs=[vmem] * 7,
        out_specs=[vmem, vmem, anywhere, anywhere],
        out_shape=[
            jax.ShapeDtypeStruct((heads, length, 128), BF),
            jax.ShapeDtypeStruct((2 * length, 128), BF),
            jax.ShapeDtypeStruct((n,) + cache.shape, cache.dtype),
            jax.ShapeDtypeStruct(gates.shape, gates.dtype),
        ],
        scratch_shapes=[
            pltpu.VMEM((rows, width), BF),
            pltpu.VMEM((length // rows, rows, width), BF),
            pltpu.VMEM((length, 128), F32),
            pltpu.VMEM((length, 128), F32),
            dma((t,)),
            dma((t,)),
            dma((r,)),
            dma((r,)),
            dma((n,)),
            dma((n,)),
            dma((length // rows,)),
            dma((length // rows,)),
            dma((2,)),
        ],
        compiler_params=pltpu.CompilerParams(
            collective_id=collective_id, has_side_effects=True, vmem_limit_bytes=VMEM_CAP
        ),
        name="opening",
    )(x, gain, cache, gates, w_query, w_keyval, angles)


def ring_scatter(parts, pair_land, land, rows, sends, receives, keys):
    place, head = lax.axis_index("tok"), lax.axis_index("head")
    started = []
    low, high = pl.ds(0, rows // 2), pl.ds(rows // 2, rows // 2)

    def spot(key):
        kind, value = key
        if kind == "far":
            return head_of(head, 2), (low if value == 1 else high)
        if kind == "plain":
            return head_of(head, value), (high if value == 1 else low)
        return head_of(head, value), (low if value == 1 else high)

    def copy(key):
        kind, value = key
        if kind == "pair":
            src, dst = parts.at[head_of(head, value, 1)], pair_land.at[keys[key]]
            peer = head_of(head, 0, 1)
        else:
            slot, rows_of = spot(key)
            src, dst = parts.at[slot, rows_of], land.at[keys[key] - 4]
            peer = head_of(head, value)
        return pltpu.make_async_remote_copy(
            src_ref=src,
            dst_ref=dst,
            send_sem=sends.at[keys[key]],
            recv_sem=receives.at[keys[key]],
            device_id=(place, peer),
            device_id_type=MESH_ID,
        )

    def send(*key):
        c = copy(key)
        c.start()
        started.append(c)

    def add(key, slot, rows_of, buffer, index):
        copy(key).wait_recv()
        parts[slot, rows_of] = (parts[slot, rows_of].astype(F32) + buffer[index].astype(F32)).astype(parts.dtype)

    def add_pair(dz):
        key = ("pair", dz)
        add(key, head_of(head, dz), pl.ds(0, rows), pair_land, keys[key])

    for dz in (2, 1, -1, 0):
        send("pair", dz)
    add_pair(2)
    for sign in (1, -1):
        send("far", sign)
    for sign in (1, -1):
        add_pair(sign)
        send("plain", sign)
    add_pair(0)
    for sign in (1, -1):
        key = ("far", sign)
        slot, rows_of = spot(("added", sign))
        add(key, slot, rows_of, land, keys[key] - 4)
        send("added", sign)
    for kind in ("plain", "added"):
        for sign in (1, -1):
            key = (kind, sign)
            _, rows_of = spot(key)
            add(key, head, rows_of, land, keys[key] - 4)
    for c in started:
        c.wait_send()


def settle_kernel(
    part_ref, tokens_ref, gain_ref, hidden_ref, out_ref, parts, pair_land, land, normed, rs, rr, ts, tr, own_sems
):
    place, head = lax.axis_index("tok"), lax.axis_index("head")
    rows = tokens_ref.shape[0]
    loads = [
        pltpu.make_async_copy(part_ref.at[pl.ds(h * rows, rows)], parts.at[h], own_sems.at[h]) for h in range(8)
    ]
    for c in loads:
        c.start()
    greet(torus_peers() + ring_peers())
    for c in loads:
        c.wait()
    ring_scatter(parts, pair_land, land, rows, rs, rr, SCATTER_RING)
    hidden = tokens_ref[...].astype(F32) + parts[head].astype(F32)
    hidden_ref[...] = hidden
    normed[...] = rms_scale(hidden, gain_ref[...].reshape(1, -1)).astype(normed.dtype)
    mine = pltpu.make_async_copy(normed, out_ref.at[place], own_sems.at[8])
    mine.start()
    for _ in torus_gather(normed, out_ref, rows, ts, tr, torus_messages()):
        pass
    mine.wait()


def settle(partial, tokens, gain, collective_id):
    rows, width = tokens.shape
    t, r = len(torus_messages()), len(SCATTER_RING)
    dma = pltpu.SemaphoreType.DMA
    return pl.pallas_call(
        settle_kernel,
        in_specs=[
            pl.BlockSpec(memory_space=pl.ANY),
            pl.BlockSpec(memory_space=pltpu.VMEM),
            pl.BlockSpec(memory_space=pltpu.VMEM),
        ],
        out_specs=[pl.BlockSpec(memory_space=pltpu.VMEM), pl.BlockSpec(memory_space=pl.ANY)],
        out_shape=[
            jax.ShapeDtypeStruct((rows, width), F32),
            jax.ShapeDtypeStruct((16, rows, width), BF),
        ],
        scratch_shapes=[
            pltpu.VMEM((8, rows, width), BF),
            pltpu.VMEM((4, rows, width), BF),
            pltpu.VMEM((6, rows // 2, width), BF),
            pltpu.VMEM((rows, width), BF),
            dma((r,)),
            dma((r,)),
            dma((t,)),
            dma((t,)),
            dma((9,)),
        ],
        compiler_params=pltpu.CompilerParams(
            collective_id=collective_id, has_side_effects=True, vmem_limit_bytes=VMEM_CAP
        ),
        name="settle",
    )(partial, tokens, gain)


def local(
    tokens,
    segments,
    group_ids,
    prefix_owner,
    slab_fill,
    prefix_cache,
    attn_gain,
    w_query,
    w_keyval,
    w_out,
    ffn_gain,
    routes,
    route_gates,
    w_gate,
    w_up,
    w_down,
):
    tok_count = lax.axis_size("tok")
    head_count = lax.axis_size("head")
    place = lax.axis_index("tok")
    row_len = tokens.shape[0] * head_count
    exp_local = w_gate.shape[0]
    experts = jnp.arange(EXPERTS, dtype=jnp.int32)[:, None, None]
    gates = jnp.sum(jnp.where(routes.T[None] == experts, route_gates.T[None], 0.0), axis=1)
    gates = gates.reshape(tok_count, exp_local, -1)
    gates = jnp.concatenate([gates, jnp.zeros((tok_count, 8 - exp_local, gates.shape[2]), F32)], axis=1)

    padded = jnp.concatenate([jnp.full((row_len,), -1, jnp.int32), segments])
    window = lax.dynamic_slice_in_dim(padded, place * row_len, 2 * row_len, 0)
    own = window[row_len:]
    begins, slabs, fills = request_tables(window, own, group_ids, prefix_owner, slab_fill)
    positions = fills + row_len + jnp.arange(row_len, dtype=jnp.int32) - begins
    steps_idx = jnp.arange(HS // 2, dtype=F32)
    inverse = jnp.exp(steps_idx * (-2.0 * jnp.log(10000.0) / HS))
    angles = inverse[:, None] * positions.astype(F32)[None, :]
    turns = jnp.concatenate([jnp.cos(angles), jnp.sin(angles)], axis=0)
    q, near, cache, gates_all = opening(tokens, attn_gain, prefix_cache, gates, w_query.T, w_keyval, turns, 1)
    cache = cache.reshape(-1, cache.shape[-1])

    span = 128
    blocks = row_len // span
    first_begin = begins.reshape(blocks, span)[:, 0]
    ends = row_len + jnp.arange(blocks, dtype=jnp.int32) * span
    steps = jnp.maximum(ends - first_begin + 2 * span - 1, 0) // (2 * span)
    ids = jnp.arange(tok_count, dtype=jnp.int32)
    present = jnp.max((slabs.reshape(blocks, span)[:, :, None] == ids).astype(jnp.int32), axis=1)
    earlier = jnp.sum(jnp.where(ids[:, None] < ids[None, :], present[:, :, None], 0), axis=1)
    listed = (present[:, None, :] == 1) & (earlier[:, None, :] == ids[None, :, None])
    used = jnp.sum(jnp.where(listed, ids, 0), axis=2)
    used = jnp.concatenate([jnp.sum(present, axis=1, keepdims=True), used], axis=1)
    rows = jnp.concatenate([begins[None], slabs[None], jnp.zeros((6, row_len), jnp.int32)], axis=0)

    partial = attend(q, near, cache, rows, steps, used, slab_fill, w_out)
    hidden, arrived = settle(partial, tokens, ffn_gain, 2)
    return run_experts(arrived, gates_all, w_gate, w_up, w_down, hidden, 3)


def solution(mesh):
    return jax.shard_map(
        local,
        mesh=mesh,
        in_specs=(
            P(("tok", "head"), None),
            P(),
            P(),
            P(),
            P(),
            P("tok", "head"),
            P(),
            P(None, "head"),
            P(None, "head"),
            P("head", None),
            P(),
            P(("tok", "head"), None),
            P(("tok", "head"), None),
            P("tok", None, None),
            P("tok", None, None),
            P("tok", None, None),
        ),
        out_specs=P(("tok", "head"), None),
        check_vma=False,
    )
```
